512 devices in a mesh: tile: 128 (over y, z_hi, x), head: 4 (over z_lo, core).
Axes of the slice: x: 4, y: 8, z: 8 (z_hi: 4, z_lo: 2; z = z_hi * 2 + z_lo), core: 2. Of those that a mesh axis runs over, the one named last changes fastest.
Arguments:
- queries: bfloat16 [32768, 1024], P('tile', 'head'), may hold values from -6 to 6
- keys: bfloat16 [32768, 1024], P('tile', 'head'), may hold values from -6 to 6
- values: bfloat16 [32768, 1024], P('tile', 'head'), may hold values from -6 to 6
- grad_output: bfloat16 [32768, 1024], P('tile', 'head'), may hold values from -24 to 24
- out_weight: bfloat16 [1024, 1024], P(None, 'head'), may hold values from -0.1875 to 0.1875
- rotations: int32 [128, 4], P('tile'), may hold values from 0 to 3, as said below
Outputs:
- grad_queries: bfloat16 [32768, 1024], P('tile', 'head')
- grad_keys: bfloat16 [32768, 1024], P('tile', 'head')
- grad_values: bfloat16 [32768, 1024], P('tile', 'head')
- grad_out_weight: float32 [1024, 1024], P('tile', 'head')
The draws below stay inside these ranges and needn't reach their ends.
Inputs may be any that keep to these rules, and one draw needn't show every extreme that they name: The tiles form 4 rows of 32 in row-major order, grouped into faces of max(8, 2) whole columns; rotations[t, s] is 0 unless side s of tile t crosses a seam, that is an east or west side between two faces or a north or south side between the last and the first row. Across a seam the two facing sides hold r and (4 - r) mod 4 with r equal to 1 or 3.
All inputs are finite; a program needn't handle non-finite values.
Results may differ from the reference program's by a relative error of at most 0.012.
Values may be sent and summed in bfloat16 or wider, within the bound.
A program may use at most 64 MiB of HBM per device.

```python
import functools
import math
import jax
import jax.numpy as jnp
from jax import lax

D = 1024
HEAD_DIM = 64
RADIUS = 6
SIDE = 16
TOKENS = 32768
N_TILE = 128


def query_key_pair(key):
    base = jax.random.fold_in(key, 4242)
    first, second = jax.random.split(base, 2)
    shape = (TOKENS, D)
    query_part = jnp.clip(jax.random.normal(first, shape, jnp.float32), -6.0, 6.0)
    key_part = jnp.clip(jax.random.normal(second, shape, jnp.float32), -6.0, 6.0)
    return (query_part, key_part)


def draw_queries(key, part):
    return query_key_pair(key)[0].astype(jnp.bfloat16)


def draw_keys(key, part):
    return query_key_pair(key)[1].astype(jnp.bfloat16)


def draw_rotations(key, part):
    columns = N_TILE // 4
    face_cols = max(N_TILE // 16, 2)
    base = jax.random.fold_in(key, 7717)
    east_key, south_key = jax.random.split(base, 2)
    east_table = jax.random.randint(east_key, (N_TILE,), 0, 2, dtype=jnp.int32) * 2 + 1
    south_table = jax.random.randint(south_key, (N_TILE,), 0, 2, dtype=jnp.int32) * 2 + 1
    tiles = jnp.arange(N_TILE, dtype=jnp.int32)
    column = tiles % columns
    west_tile = (tiles - 1) % N_TILE
    north_tile = (tiles - columns) % N_TILE
    east_seam = (column + 1) % face_cols == 0
    west_seam = (west_tile % columns + 1) % face_cols == 0
    south_seam = tiles >= N_TILE - columns
    north_seam = tiles < columns
    zero = jnp.zeros((N_TILE,), jnp.int32)
    east = jnp.where(east_seam, east_table, zero)
    west = jnp.where(west_seam, (4 - east_table[west_tile]) % 4, zero)
    south = jnp.where(south_seam, south_table, zero)
    north = jnp.where(north_seam, (4 - south_table[north_tile]) % 4, zero)
    return jnp.stack([north, east, south, west], axis=1).astype(jnp.int32)


def raised(array, key, source, target, shards_of, factor):
    owner, partner = [(jnp.arange(array.shape[dim]) // (array.shape[dim] // shards_of)).reshape([-1 if axis == dim else 1 for axis in range(array.ndim)]) for dim in (source, target)]
    chosen = jax.random.permutation(key, shards_of)[partner]
    strong = (owner == chosen) | (owner == (partner + shards_of // 2) % shards_of)
    return jnp.where(strong, factor * array, array)


def block_scale(key, dims, cuts, least, largest):
    level, own = 1.0, jax.random.fold_in(key, 6)
    for axis_at, blocks in cuts:
        heights = jnp.exp(jax.random.uniform(jax.random.fold_in(own, axis_at), (blocks,), jnp.float32, least / len(cuts), largest / len(cuts)))
        level = level * jnp.repeat(heights, dims[axis_at] // blocks).reshape([-1 if axis == axis_at else 1 for axis in range(len(dims))])
    return level


def noise(stream_key, shape, spread, limit, cuts=(), kind=jnp.bfloat16):
    level = block_scale(stream_key, shape, cuts, -0.22, 0.18) if cuts else 1.0
    array = jax.random.normal(stream_key, shape, jnp.float32) * spread * level
    return jnp.minimum(jnp.maximum(array, -limit), limit).astype(kind)


def heavy_noise(rng, shape, width, bound, cuts, heavy, kind=jnp.bfloat16):
    values = width * jax.random.normal(rng, shape, jnp.float32)
    if cuts:
        values = values * block_scale(rng, shape, cuts, -0.22, 0.18)
    return jnp.clip(raised(values, jax.random.fold_in(rng, 3), *heavy), -bound, bound).astype(kind)


def setup_inputs(seed: int = 0) -> dict:
    splits = jax.random.split(jax.random.key(seed), 7)
    queries = draw_queries(jax.random.fold_in(splits[6], 71), 0)
    keys = draw_keys(jax.random.fold_in(splits[6], 71), 0)
    values = noise(splits[2], (TOKENS, D), 1.0, 6.0, ((0, 128), (1, 4)))
    grad_output = heavy_noise(splits[3], (TOKENS, D), 1.0, 24.0, ((0, 128), (1, 4)), (0, 1, 128, 5.5))
    out_weight = noise(splits[4], (D, D), D ** -0.5, 0.1875, ((1, 4),))
    rotations = draw_rotations(jax.random.fold_in(splits[6], 71), 0)
    return {"queries": queries, "keys": keys, "values": values, "grad_output": grad_output, "out_weight": out_weight, "rotations": rotations}


def turned_rim(tile_grid, number):
    return jnp.rot90(tile_grid, number)[tile_grid.shape[0] - RADIUS:]

def rim_strip(tile_grid, turn_count):
    branches = [functools.partial(turned_rim, number=number) for number in range(4)]
    return lax.switch(turn_count, branches, tile_grid)

def placed_back(strip, number, tile_side):
    padded = jnp.pad(strip, ((tile_side - RADIUS, 0), (0, 0), (0, 0)))
    return jnp.rot90(padded, -number)

def place_back(strip, turn_count, tile_side):
    branches = [functools.partial(placed_back, number=number, tile_side=tile_side) for number in range(4)]
    return lax.switch(turn_count, branches, strip)

def extend(tile_grid, strips):
    tile_side = tile_grid.shape[0]
    extended = jnp.pad(tile_grid, ((RADIUS, RADIUS), (RADIUS, RADIUS), (0, 0)))
    for side_index in range(4):
        turned = jnp.rot90(extended, side_index)
        turned = turned.at[:RADIUS, RADIUS:RADIUS + tile_side].set(strips[side_index])
        extended = jnp.rot90(turned, -side_index)
    return extended

def inner_rim(extended, side_index, tile_side):
    return jnp.rot90(extended, side_index)[:RADIUS, RADIUS:RADIUS + tile_side]

def window_backward(query_grid, key_ext, value_ext, dout_grid):
    tile_side = query_grid.shape[0]
    features = query_grid.shape[-1]
    extended = tile_side + 2 * RADIUS
    score_scale = HEAD_DIM ** (-0.5)
    query_rows = query_grid.reshape(tile_side * tile_side, features)
    dout_rows = dout_grid.reshape(tile_side * tile_side, features)
    key_rows = key_ext.reshape(extended * extended, features)
    value_rows = value_ext.reshape(extended * extended, features)
    query_index = jnp.arange(tile_side * tile_side, dtype=jnp.int32)
    query_row = query_index // tile_side + RADIUS
    query_col = query_index % tile_side + RADIUS
    cell_index = jnp.arange(extended * extended, dtype=jnp.int32)
    cell_row = cell_index // extended
    cell_col = cell_index % extended
    outer_row = (cell_row < RADIUS) | (cell_row >= RADIUS + tile_side)
    outer_col = (cell_col < RADIUS) | (cell_col >= RADIUS + tile_side)
    corner = outer_row & outer_col
    allowed = (jnp.abs(cell_row[None, :] - query_row[:, None]) <= RADIUS) & (jnp.abs(cell_col[None, :] - query_col[:, None]) <= RADIUS) & jnp.logical_not(corner)[None, :]
    attention_list = []
    grad_query_list = []
    grad_key_list = []
    grad_value_list = []
    for head_index in range(features // HEAD_DIM):
        head_cols = slice(head_index * HEAD_DIM, (head_index + 1) * HEAD_DIM)
        query_head = query_rows[:, head_cols]
        key_head = key_rows[:, head_cols]
        value_head = value_rows[:, head_cols]
        dout_head = dout_rows[:, head_cols]
        scores = lax.dot_general(query_head, key_head, (((1,), (1,)), ((), ())), preferred_element_type=jnp.float32) * score_scale
        scores = jnp.where(allowed, scores, -1e+30)
        row_max = lax.optimization_barrier(jnp.max(scores, axis=1, keepdims=True))
        raw_weights = jnp.exp(scores - row_max)
        weights = raw_weights / lax.optimization_barrier(jnp.sum(raw_weights, axis=1, keepdims=True))
        weights_bf = weights.astype(jnp.bfloat16)
        attention = jnp.dot(weights_bf, value_head, preferred_element_type=jnp.float32)
        row_delta = lax.optimization_barrier(jnp.sum(dout_head.astype(jnp.float32) * attention, axis=1, keepdims=True))
        grad_weights = lax.dot_general(dout_head, value_head, (((1,), (1,)), ((), ())), preferred_element_type=jnp.float32)
        dscore = (weights * (grad_weights - row_delta)).astype(jnp.bfloat16)
        grad_query = jnp.dot(dscore, key_head, preferred_element_type=jnp.float32) * score_scale
        grad_key = lax.dot_general(dscore, query_head, (((0,), (0,)), ((), ())), preferred_element_type=jnp.float32) * score_scale
        grad_value = lax.dot_general(weights_bf, dout_head, (((0,), (0,)), ((), ())), preferred_element_type=jnp.float32)
        attention_list.append(attention)
        grad_query_list.append(grad_query)
        grad_key_list.append(grad_key)
        grad_value_list.append(grad_value)
    attention_all = jnp.concatenate(attention_list, axis=1)
    grad_query_all = jnp.concatenate(grad_query_list, axis=1)
    grad_key_all = jnp.concatenate(grad_key_list, axis=1).reshape(extended, extended, features)
    grad_value_all = jnp.concatenate(grad_value_list, axis=1).reshape(extended, extended, features)
    return (attention_all, grad_query_all, grad_key_all, grad_value_all)

def reference(queries, keys, values, grad_output, out_weight, rotations):
    tile_count = N_TILE
    features = D
    tile_side = SIDE
    dout = jnp.dot(grad_output, out_weight, preferred_element_type=jnp.float32).astype(jnp.bfloat16)
    query_tiles = queries.reshape(tile_count, tile_side, tile_side, features)
    dout_tiles = dout.reshape(tile_count, tile_side, tile_side, features)
    pair_tiles = jnp.concatenate([keys, values], axis=1).reshape(tile_count, tile_side, tile_side, 2 * features)
    offsets = (-(tile_count // 4), 1, tile_count // 4, -1)
    tile_numbers = jnp.arange(tile_count, dtype=jnp.int32)

    def one_tile(tile_index):
        strips = []
        for side_index in range(4):
            neighbour = (tile_index + offsets[side_index]) % tile_count
            turn_count = ((side_index + rotations[tile_index, side_index]) % 4).astype(jnp.int32)
            strips.append(rim_strip(pair_tiles[neighbour], turn_count))
        extended = extend(pair_tiles[tile_index], strips)
        attention, grad_query, grad_key, grad_value = window_backward(query_tiles[tile_index], extended[..., :features], extended[..., features:], dout_tiles[tile_index])
        grad_pair = jnp.concatenate([grad_key, grad_value], axis=-1)
        centre = grad_pair[RADIUS:RADIUS + tile_side, RADIUS:RADIUS + tile_side]
        backs = jnp.stack([inner_rim(grad_pair, side_index, tile_side) for side_index in range(4)])
        return (attention.astype(jnp.bfloat16), grad_query.astype(jnp.bfloat16), centre, backs)
    attention_bf, grad_query, centres, backs = lax.map(one_tile, tile_numbers)

    def owner(tile_index):
        total = centres[tile_index]
        for side_index in range(4):
            source = (tile_index - offsets[side_index]) % tile_count
            turn_count = ((side_index + rotations[source, side_index]) % 4).astype(jnp.int32)
            total = total + place_back(backs[source, side_index], turn_count, tile_side)
        return total.astype(jnp.bfloat16)
    grad_pair = lax.map(owner, tile_numbers)
    grad_keys = grad_pair[..., :features].reshape(TOKENS, features)
    grad_values = grad_pair[..., features:].reshape(TOKENS, features)
    grad_queries = grad_query.reshape(TOKENS, features)
    attention_rows = attention_bf.reshape(TOKENS, features)
    grad_out_weight = lax.dot_general(grad_output, attention_rows, (((0,), (0,)), ((), ())), preferred_element_type=jnp.float32) * (1.0 / math.sqrt(TOKENS))
    return (grad_queries, grad_keys, grad_values, grad_out_weight)
```

```python
import functools
import math

import jax
import jax.numpy as jnp
from jax import lax
from jax.experimental import pallas as pl
from jax.experimental.pallas import tpu as pltpu
from jax.sharding import PartitionSpec as P

HEAD_DIM = 64
RADIUS = 6
SIDE = 16
CELLS = SIDE * SIDE
STRIP = RADIUS * SIDE
EXT = CELLS + 4 * STRIP
MESH = pl.DeviceIdType.MESH
BF = jnp.bfloat16
F32 = jnp.float32
NT = (((1,), (1,)), ((), ()))


def dot(a, b):
    return jnp.dot(a, b, preferred_element_type=F32)


def dot_nt(a, b):
    return lax.dot_general(a, b, NT, preferred_element_type=F32)


def tile_axes(tile_count):
    return {128: (8, 4, 4), 8: (2, 2, 2)}[tile_count]


def kernel(
    tile_count,
    q_hbm,
    k_hbm,
    v_hbm,
    g_hbm,
    w_hbm,
    rot_ref,
    gq_hbm,
    gk_hbm,
    gv_hbm,
    gow_hbm,
    qbuf,
    kv,
    gbuf,
    gturned,
    wbuf,
    pick,
    pick_turned,
    strips,
    bias,
    qstack,
    kvt,
    weights,
    weights_bf,
    dscore,
    att_t,
    dstack,
    dturned,
    centre,
    back,
    returned,
    xsend,
    xrecv,
    ysum,
    yrecv,
    zsum,
    zrecv,
    gq_out,
    gkv_out,
    gow_out,
    gq_t,
    load_sem,
    store_sem,
    ag_send,
    ag_recv,
    halo_send,
    halo_recv,
    ret_send,
    ret_recv,
    x_send,
    x_recv,
    y_send,
    y_recv,
    z_send,
    z_recv,
):
    ny, nz, nx = tile_axes(tile_count)
    features = q_hbm.shape[1]
    heads = features // HEAD_DIM
    rows = gow_hbm.shape[0]
    t = lax.axis_index("tile")
    h = lax.axis_index("head")
    x = lax.rem(t, nx)
    z = lax.rem(t // nx, nz)
    y = t // (nx * nz)
    h1 = h + 1 - 2 * lax.rem(h, 2)
    h2 = lax.rem(h + 2, 4)
    h3 = 3 - h

    def at_xyz(yy, zz, xx):
        return (yy * nz + zz) * nx + xx

    def x_peer(k):
        return at_xyz(y, z, lax.rem(x + k, nx))

    def y_peer(k):
        return at_xyz(lax.rem(y + k, ny), z, x)

    def z_peer(k):
        return at_xyz(y, lax.rem(z + k, nz), x)

    offsets = (-(tile_count // 4), 1, tile_count // 4, -1)

    def beside(side):
        return lax.rem(t + offsets[side] + tile_count, tile_count)

    loads = [
        pltpu.make_async_copy(k_hbm, kv.at[0:CELLS, 0:features], load_sem.at[0]),
        pltpu.make_async_copy(v_hbm, kv.at[0:CELLS, features : 2 * features], load_sem.at[1]),
        pltpu.make_async_copy(q_hbm, qbuf, load_sem.at[2]),
        pltpu.make_async_copy(g_hbm, gbuf.at[0], load_sem.at[3]),
        pltpu.make_async_copy(w_hbm, wbuf, load_sem.at[4]),
    ]
    barrier = pltpu.get_barrier_semaphore()
    peers = [(t, h1), (t, h2), (t, h3)]
    peers += [(beside(side), h) for side in range(4)]
    peers += [(y_peer(k), h) for k in range(1, ny)]
    peers += [(x_peer(k), h) for k in range(1, nx)]
    peers += [(z_peer(k), h) for k in range(1, nz)]
    for peer in peers:
        pl.semaphore_signal(barrier, inc=1, device_id=peer, device_id_type=MESH)
    for load in loads:
        load.start()

    starts, down, along = [], [], []
    for side in range(4):
        turn = lax.rem(side + 4 - rot_ref[0, (side + 2) % 4], 4)

        def choose(a, b, c, d, turn=turn):
            return jnp.where(turn == 0, a, jnp.where(turn == 1, b, jnp.where(turn == 2, c, d)))

        starts.append(choose(160, 5, 95, 250))
        down.append(choose(16, -1, -16, 1))
        along.append(choose(1, 16, -1, -16))
    place = lax.broadcasted_iota(jnp.int32, (STRIP, CELLS), 0)
    cell = lax.broadcasted_iota(jnp.int32, (STRIP, CELLS), 1)
    for side in range(4):
        target = starts[side] + down[side] * (place // SIDE) + along[side] * (place % SIDE)
        pick[side * STRIP : (side + 1) * STRIP, :] = jnp.where(cell == target, 1.0, 0.0).astype(BF)
    loads[0].wait()
    loads[1].wait()
    strips[...] = dot(pick[...], kv[0:CELLS, :]).astype(BF)

    halos = [
        pltpu.make_async_remote_copy(
            src_ref=strips.at[side * STRIP : (side + 1) * STRIP],
            dst_ref=kv.at[CELLS + side * STRIP : CELLS + (side + 1) * STRIP],
            send_sem=halo_send.at[side],
            recv_sem=halo_recv.at[side],
            device_id=(beside((side + 2) % 4), h),
            device_id_type=MESH,
        )
        for side in range(4)
    ]
    gathers = [
        pltpu.make_async_remote_copy(
            src_ref=source,
            dst_ref=gbuf.at[slot],
            send_sem=ag_send.at[slot - 1],
            recv_sem=ag_recv.at[slot - 1],
            device_id=(t, peer),
            device_id_type=MESH,
        )
        for slot, source, peer in ((1, g_hbm, h1), (2, g_hbm, h2), (3, gbuf.at[2], h1))
    ]
    pl.semaphore_wait(barrier, len(peers))
    for halo in halos:
        halo.start()
    gathers[1].start()
    gathers[0].start()

    cell_t = lax.broadcasted_iota(jnp.int32, (CELLS, 4 * STRIP), 0)
    place_t = lax.broadcasted_iota(jnp.int32, (CELLS, 4 * STRIP), 1)
    side_t = place_t // STRIP
    rest_t = place_t - side_t * STRIP

    def by_side(values):
        return jnp.where(
            side_t == 0,
            values[0],
            jnp.where(side_t == 1, values[1], jnp.where(side_t == 2, values[2], values[3])),
        )

    target_t = by_side(starts) + by_side(down) * (rest_t // SIDE) + by_side(along) * (rest_t % SIDE)
    pick_turned[...] = jnp.where(cell_t == target_t, 1.0, 0.0).astype(BF)

    def fill_bias(first, count, where_is):
        index = lax.broadcasted_iota(jnp.int32, (count, CELLS), 0)
        query = lax.broadcasted_iota(jnp.int32, (count, CELLS), 1)
        a, b = where_is(index // SIDE, index % SIDE)
        off_a = a - query // SIDE
        off_b = b - query % SIDE
        inside = (off_a >= 0) & (off_a <= 2 * RADIUS) & (off_b >= 0) & (off_b <= 2 * RADIUS)
        bias[first : first + count, :] = jnp.where(inside, 0.0, -1e30)

    last = SIDE + 2 * RADIUS - 1
    fill_bias(0, CELLS, lambda i, j: (i + RADIUS, j + RADIUS))
    fill_bias(CELLS, STRIP, lambda i, j: (i, RADIUS + j))
    fill_bias(CELLS + STRIP, STRIP, lambda i, j: (RADIUS + j, last - i))
    fill_bias(CELLS + 2 * STRIP, STRIP, lambda i, j: (last - i, last - RADIUS - j))
    fill_bias(CELLS + 3 * STRIP, STRIP, lambda i, j: (last - RADIUS - j, i))

    loads[2].wait()
    lane = lax.broadcasted_iota(jnp.int32, (CELLS, features), 1)
    scaled = qbuf[...].astype(F32) * (HEAD_DIM ** (-0.5))
    for head in range(heads):
        own = lane // HEAD_DIM == head
        qstack[head * CELLS : (head + 1) * CELLS, :] = jnp.where(own, scaled, 0.0).astype(BF)

    gathers[1].wait_recv()
    gathers[2].start()
    loads[3].wait()
    gturned[0] = gbuf[0].T
    gturned[2] = gbuf[2].T
    gathers[0].wait_recv()
    gturned[1] = gbuf[1].T
    for halo in halos:
        halo.wait_recv()
    kvt[...] = kv[...].T
    gathers[2].wait_recv()
    gturned[3] = gbuf[3].T

    pieces = 5
    piece = EXT // pieces
    for head in range(heads):
        cols = slice(head * CELLS, (head + 1) * CELLS)
        score = dot_nt(kv[:, 0:features], qstack[cols, :])
        top = None
        for n in range(pieces):
            part = slice(n * piece, (n + 1) * piece)
            masked = score[part] + bias[part, :]
            weights[part, cols] = masked
            highest = jnp.max(masked.reshape(piece // 8, 8, CELLS), axis=0)
            top = highest if top is None else jnp.maximum(top, highest)
        top = jnp.max(top, axis=0, keepdims=True)
        total = None
        for n in range(pieces):
            part = slice(n * piece, (n + 1) * piece)
            raw = jnp.exp(weights[part, cols] - top)
            weights[part, cols] = raw
            summed = jnp.sum(raw.reshape(piece // 8, 8, CELLS), axis=0)
            total = summed if total is None else total + summed
        inverse = 1.0 / jnp.sum(total, axis=0, keepdims=True)
        for n in range(pieces):
            part = slice(n * piece, (n + 1) * piece)
            normal = weights[part, cols] * inverse
            weights[part, cols] = normal
            weights_bf[part, cols] = normal.astype(BF)
        own_rows = slice(head * HEAD_DIM, (head + 1) * HEAD_DIM)
        att_t[own_rows, :] = dot(
            kvt[features + head * HEAD_DIM : features + (head + 1) * HEAD_DIM, :],
            weights_bf[:, cols],
        )
    att_bf = att_t[...].astype(BF)

    holders = (h, h1, h2, h3)
    per_slot = features // rows // nx * rows
    for slot in range(4):
        term = dot_nt(gturned[slot], att_bf)
        term = term.reshape(per_slot // rows, nx, rows, features)
        for xx in range(nx):
            first = pl.multiple_of(holders[slot] * per_slot, per_slot)
            xsend[xx, pl.ds(first, per_slot), :] = (
                term[:, xx].reshape(per_slot, features).astype(BF)
            )
    x_copies = [
        pltpu.make_async_remote_copy(
            src_ref=xsend.at[lax.rem(x + k, nx)],
            dst_ref=xrecv.at[k - 1],
            send_sem=x_send.at[k - 1],
            recv_sem=x_recv.at[k - 1],
            device_id=(x_peer(k), h),
            device_id_type=MESH,
        )
        for k in range(1, nx)
    ]
    for copy in x_copies:
        copy.start()

    loads[4].wait()
    dout = None
    for slot in range(4):
        first = pl.multiple_of(holders[slot] * features, features)
        term = dot(gbuf[slot], wbuf[pl.ds(first, features), :])
        dout = term if dout is None else dout + term
    dout_bf = dout.astype(BF)
    dout = dout_bf.astype(F32)
    dout_t = dout.T
    row = lax.broadcasted_iota(jnp.int32, (features, CELLS), 0)
    product = dout_t * att_t[...]
    for head in range(heads):
        own = lane // HEAD_DIM == head
        dstack[head * CELLS : (head + 1) * CELLS, :] = jnp.where(own, dout, 0.0).astype(BF)
        own = row // HEAD_DIM == head
        dturned[head * features : (head + 1) * features, :] = jnp.where(own, dout_t, 0.0).astype(BF)
    for head in range(heads):
        cols = slice(head * CELLS, (head + 1) * CELLS)
        own_rows = slice(head * HEAD_DIM, (head + 1) * HEAD_DIM)
        delta = jnp.sum(product[own_rows], axis=0, keepdims=True)
        grad_weight = dot(kv[:, features : 2 * features], dturned[head * features : (head + 1) * features, :])
        for n in range(pieces):
            part = slice(n * piece, (n + 1) * piece)
            dscore[part, cols] = (weights[part, cols] * (grad_weight[part] - delta)).astype(BF)
        gq_t[own_rows, :] = dot(kvt[own_rows, :], dscore[:, cols])
    back[:, 0:features] = dot(dscore[CELLS:EXT, :], qstack[...]).astype(BF)
    back[:, features : 2 * features] = dot(weights_bf[CELLS:EXT, :], dstack[...]).astype(BF)
    returns = [
        pltpu.make_async_remote_copy(
            src_ref=back.at[side * STRIP : (side + 1) * STRIP],
            dst_ref=returned.at[side * STRIP : (side + 1) * STRIP],
            send_sem=ret_send.at[side],
            recv_sem=ret_recv.at[side],
            device_id=(beside(side), h),
            device_id_type=MESH,
        )
        for side in range(4)
    ]
    for copy in returns:
        copy.start()
    centre[:, 0:features] = dot(dscore[0:CELLS, :], qstack[...])
    centre[:, features : 2 * features] = dot(weights_bf[0:CELLS, :], dstack[...])
    gq_out[...] = (gq_t[...].T * (HEAD_DIM ** (-0.5))).astype(BF)
    stores = [pltpu.make_async_copy(gq_out, gq_hbm, store_sem.at[0])]
    stores[0].start()

    for copy in x_copies:
        copy.wait_recv()
    total = xsend[x].astype(F32)
    for k in range(nx - 1):
        total = total + xrecv[k].astype(F32)
    ysum[...] = total.astype(BF)
    block = nz * rows
    y_copies = [
        pltpu.make_async_remote_copy(
            src_ref=ysum.at[pl.ds(pl.multiple_of(lax.rem(y + k, ny) * block, block), block)],
            dst_ref=yrecv.at[k - 1],
            send_sem=y_send.at[k - 1],
            recv_sem=y_recv.at[k - 1],
            device_id=(y_peer(k), h),
            device_id_type=MESH,
        )
        for k in range(1, ny)
    ]
    for copy in y_copies:
        copy.start()

    for copy in returns:
        copy.wait_recv()
    gkv_out[...] = (centre[...] + dot(pick_turned[...], returned[...])).astype(BF)
    stores.append(pltpu.make_async_copy(gkv_out.at[:, 0:features], gk_hbm, store_sem.at[1]))
    stores.append(
        pltpu.make_async_copy(gkv_out.at[:, features : 2 * features], gv_hbm, store_sem.at[2])
    )
    stores[1].start()
    stores[2].start()

    for copy in y_copies:
        copy.wait_recv()
    total = ysum[pl.ds(pl.multiple_of(y * block, block), block), :].astype(F32)
    for k in range(ny - 1):
        total = total + yrecv[k].astype(F32)
    zsum[...] = total
    z_copies = [
        pltpu.make_async_remote_copy(
            src_ref=zsum.at[pl.ds(pl.multiple_of(lax.rem(z + k, nz) * rows, rows), rows)],
            dst_ref=zrecv.at[k - 1],
            send_sem=z_send.at[k - 1],
            recv_sem=z_recv.at[k - 1],
            device_id=(z_peer(k), h),
            device_id_type=MESH,
        )
        for k in range(1, nz)
    ]
    for copy in z_copies:
        copy.start()
    for copy in z_copies:
        copy.wait_recv()
    total = zsum[pl.ds(pl.multiple_of(z * rows, rows), rows), :]
    for k in range(nz - 1):
        total = total + zrecv[k]
    gow_out[...] = total * (1.0 / math.sqrt(CELLS * tile_count))
    stores.append(pltpu.make_async_copy(gow_out, gow_hbm, store_sem.at[3]))
    stores[3].start()
    for copy in halos + gathers + x_copies + returns + y_copies + z_copies:
        copy.wait_send()
    for store in stores:
        store.wait()


def shards(queries, keys, values, grad_output, out_weight, rotations):
    tile_count = lax.axis_size("tile")
    tokens, features = queries.shape
    heads = features // HEAD_DIM
    width = out_weight.shape[0]
    rows = width // tile_count
    ny, nz, nx = tile_axes(tile_count)
    anywhere = pl.BlockSpec(memory_space=pl.ANY)
    out = jax.ShapeDtypeStruct((tokens, features), BF)
    dma = pltpu.SemaphoreType.DMA
    return pl.pallas_call(
        functools.partial(kernel, tile_count),
        out_shape=(out, out, out, jax.ShapeDtypeStruct((rows, features), F32)),
        in_specs=[anywhere] * 5 + [pl.BlockSpec(memory_space=pltpu.SMEM)],
        out_specs=(anywhere,) * 4,
        scratch_shapes=[
            pltpu.VMEM((CELLS, features), BF),
            pltpu.VMEM((EXT, 2 * features), BF),
            pltpu.VMEM((4, CELLS, features), BF),
            pltpu.VMEM((4, features, CELLS), BF),
            pltpu.VMEM((width, features), BF),
            pltpu.VMEM((4 * STRIP, CELLS), BF),
            pltpu.VMEM((CELLS, 4 * STRIP), BF),
            pltpu.VMEM((4 * STRIP, 2 * features), BF),
            pltpu.VMEM((EXT, CELLS), F32),
            pltpu.VMEM((heads * CELLS, features), BF),
            pltpu.VMEM((2 * features, EXT), BF),
            pltpu.VMEM((EXT, heads * CELLS), F32),
            pltpu.VMEM((EXT, heads * CELLS), BF),
            pltpu.VMEM((EXT, heads * CELLS), BF),
            pltpu.VMEM((features, CELLS), F32),
            pltpu.VMEM((heads * CELLS, features), BF),
            pltpu.VMEM((heads * features, CELLS), BF),
            pltpu.VMEM((CELLS, 2 * features), F32),
            pltpu.VMEM((4 * STRIP, 2 * features), BF),
            pltpu.VMEM((4 * STRIP, 2 * features), BF),
            pltpu.VMEM((nx, width // nx, features), BF),
            pltpu.VMEM((nx - 1, width // nx, features), BF),
            pltpu.VMEM((width // nx, features), BF),
            pltpu.VMEM((ny - 1, nz * rows, features), BF),
            pltpu.VMEM((nz * rows, features), F32),
            pltpu.VMEM((nz - 1, rows, features), F32),
            pltpu.VMEM((CELLS, features), BF),
            pltpu.VMEM((CELLS, 2 * features), BF),
            pltpu.VMEM((rows, features), F32),
            pltpu.VMEM((features, CELLS), F32),
            dma((5,)),
            dma((4,)),
            dma((3,)),
            dma((3,)),
            dma((4,)),
            dma((4,)),
            dma((4,)),
            dma((4,)),
            dma((nx - 1,)),
            dma((nx - 1,)),
            dma((ny - 1,)),
            dma((ny - 1,)),
            dma((nz - 1,)),
            dma((nz - 1,)),
        ],
        compiler_params=pltpu.CompilerParams(collective_id=0, has_side_effects=True),
    )(queries, keys, values, grad_output, out_weight, rotations)


def solution(mesh):
    placed = (
        P("tile", "head"),
        P("tile", "head"),
        P("tile", "head"),
        P("tile", "head"),
        P(None, "head"),
        P("tile", None),
    )
    return jax.shard_map(
        shards,
        mesh=mesh,
        in_specs=placed,
        out_specs=(P("tile", "head"), P("tile", "head"), P("tile", "head"), P("tile", "head")),
        check_vma=False,
    )
```

```python
import functools
import math

import jax
import jax.numpy as jnp
from jax import lax
from jax.experimental import pallas as pl
from jax.experimental.pallas import tpu as pltpu
from jax.sharding import PartitionSpec as P

HEAD_DIM = 64
RADIUS = 6
SIDE = 16
CELLS = SIDE * SIDE
STRIP = RADIUS * SIDE
EXT = CELLS + 4 * STRIP
MESH = pl.DeviceIdType.MESH
BF = jnp.bfloat16
F32 = jnp.float32
NT = (((1,), (1,)), ((), ()))


def dot(a, b):
    return jnp.dot(a, b, preferred_element_type=F32)


def dot_nt(a, b):
    return lax.dot_general(a, b, NT, preferred_element_type=F32)


def tile_axes(tile_count):
    return {128: (8, 4, 4), 8: (2, 2, 2)}[tile_count]


def kernel(
    tile_count,
    q_hbm,
    k_hbm,
    v_hbm,
    g_hbm,
    w_hbm,
    rot_ref,
    gq_hbm,
    gk_hbm,
    gv_hbm,
    gow_hbm,
    qbuf,
    kbuf,
    vbuf,
    gbuf,
    gturned,
    wbuf,
    pick,
    pick_turned,
    kstrips,
    vstrips,
    bias,
    qstack,
    kt,
    vt,
    weights,
    weights_bf,
    dscore,
    att_t,
    dstack,
    dturned,
    centre_k,
    centre_v,
    kback,
    vback,
    kreturned,
    vreturned,
    xsend,
    xrecv,
    ysum,
    yrecv,
    zsum,
    zrecv,
    gq_out,
    gk_out,
    gv_out,
    gow_out,
    gq_t,
    load_sem,
    store_sem,
    ag_send,
    ag_recv,
    halo_send,
    halo_recv,
    ret_send,
    ret_recv,
    x_send,
    x_recv,
    y_send,
    y_recv,
    z_send,
    z_recv,
):
    ny, nz, nx = tile_axes(tile_count)
    features = q_hbm.shape[1]
    heads = features // HEAD_DIM
    rows = gow_hbm.shape[0]
    t = lax.axis_index("tile")
    h = lax.axis_index("head")
    x = lax.rem(t, nx)
    z = lax.rem(t // nx, nz)
    y = t // (nx * nz)
    h1 = h + 1 - 2 * lax.rem(h, 2)
    h2 = lax.rem(h + 2, 4)
    h3 = 3 - h

    def at_xyz(yy, zz, xx):
        return (yy * nz + zz) * nx + xx

    def x_peer(k):
        return at_xyz(y, z, lax.rem(x + k, nx))

    def y_peer(k):
        return at_xyz(lax.rem(y + k, ny), z, x)

    def z_peer(k):
        return at_xyz(y, lax.rem(z + k, nz), x)

    offsets = (-(tile_count // 4), 1, tile_count // 4, -1)

    def beside(side):
        return lax.rem(t + offsets[side] + tile_count, tile_count)

    loads = [
        pltpu.make_async_copy(k_hbm, kbuf.at[0:CELLS], load_sem.at[0]),
        pltpu.make_async_copy(v_hbm, vbuf.at[0:CELLS], load_sem.at[1]),
        pltpu.make_async_copy(q_hbm, qbuf, load_sem.at[2]),
        pltpu.make_async_copy(g_hbm, gbuf.at[0], load_sem.at[3]),
        pltpu.make_async_copy(w_hbm, wbuf, load_sem.at[4]),
    ]
    barrier = pltpu.get_barrier_semaphore()
    peers = [(t, h1), (t, h2), (t, h3)]
    peers += [(beside(side), h) for side in range(4)]
    peers += [(y_peer(k), h) for k in range(1, ny)]
    peers += [(x_peer(k), h) for k in range(1, nx)]
    peers += [(z_peer(k), h) for k in range(1, nz)]
    for peer in peers:
        pl.semaphore_signal(barrier, inc=1, device_id=peer, device_id_type=MESH)
    for load in loads:
        load.start()

    starts, down, along = [], [], []
    for side in range(4):
        turn = lax.rem(side + 4 - rot_ref[0, (side + 2) % 4], 4)

        def choose(a, b, c, d, turn=turn):
            return jnp.where(turn == 0, a, jnp.where(turn == 1, b, jnp.where(turn == 2, c, d)))

        starts.append(choose(160, 5, 95, 250))
        down.append(choose(16, -1, -16, 1))
        along.append(choose(1, 16, -1, -16))
    place = lax.broadcasted_iota(jnp.int32, (STRIP, CELLS), 0)
    cell = lax.broadcasted_iota(jnp.int32, (STRIP, CELLS), 1)
    for side in range(4):
        target = starts[side] + down[side] * (place // SIDE) + along[side] * (place % SIDE)
        pick[side * STRIP : (side + 1) * STRIP, :] = jnp.where(cell == target, 1.0, 0.0).astype(BF)
    loads[0].wait()
    kstrips[...] = dot(pick[...], kbuf[0:CELLS, :]).astype(BF)
    loads[1].wait()
    vstrips[...] = dot(pick[...], vbuf[0:CELLS, :]).astype(BF)

    def halo(number, source, target, side):
        return pltpu.make_async_remote_copy(
            src_ref=source.at[side * STRIP : (side + 1) * STRIP],
            dst_ref=target.at[CELLS + side * STRIP : CELLS + (side + 1) * STRIP],
            send_sem=halo_send.at[number, side],
            recv_sem=halo_recv.at[number, side],
            device_id=(beside((side + 2) % 4), h),
            device_id_type=MESH,
        )

    order = (1, 3, 0, 2)
    key_halos = [halo(0, kstrips, kbuf, side) for side in order]
    value_halos = [halo(1, vstrips, vbuf, side) for side in order]
    gathers = [
        pltpu.make_async_remote_copy(
            src_ref=source,
            dst_ref=gbuf.at[slot],
            send_sem=ag_send.at[slot - 1],
            recv_sem=ag_recv.at[slot - 1],
            device_id=(t, peer),
            device_id_type=MESH,
        )
        for slot, source, peer in ((1, g_hbm, h1), (2, g_hbm, h2), (3, gbuf.at[2], h1))
    ]
    pl.semaphore_wait(barrier, len(peers))
    for copy in key_halos:
        copy.start()
    gathers[1].start()
    gathers[0].start()
    for copy in value_halos:
        copy.start()

    cell_t = lax.broadcasted_iota(jnp.int32, (CELLS, 4 * STRIP), 0)
    place_t = lax.broadcasted_iota(jnp.int32, (CELLS, 4 * STRIP), 1)
    side_t = place_t // STRIP
    rest_t = place_t - side_t * STRIP

    def by_side(values):
        return jnp.where(
            side_t == 0,
            values[0],
            jnp.where(side_t == 1, values[1], jnp.where(side_t == 2, values[2], values[3])),
        )

    target_t = by_side(starts) + by_side(down) * (rest_t // SIDE) + by_side(along) * (rest_t % SIDE)
    pick_turned[...] = jnp.where(cell_t == target_t, 1.0, 0.0).astype(BF)

    def fill_bias(first, count, where_is):
        index = lax.broadcasted_iota(jnp.int32, (count, CELLS), 0)
        query = lax.broadcasted_iota(jnp.int32, (count, CELLS), 1)
        a, b = where_is(index // SIDE, index % SIDE)
        off_a = a - query // SIDE
        off_b = b - query % SIDE
        inside = (off_a >= 0) & (off_a <= 2 * RADIUS) & (off_b >= 0) & (off_b <= 2 * RADIUS)
        bias[first : first + count, :] = jnp.where(inside, 0.0, -1e30)

    last = SIDE + 2 * RADIUS - 1
    fill_bias(0, CELLS, lambda i, j: (i + RADIUS, j + RADIUS))
    fill_bias(CELLS, STRIP, lambda i, j: (i, RADIUS + j))
    fill_bias(CELLS + STRIP, STRIP, lambda i, j: (RADIUS + j, last - i))
    fill_bias(CELLS + 2 * STRIP, STRIP, lambda i, j: (last - i, last - RADIUS - j))
    fill_bias(CELLS + 3 * STRIP, STRIP, lambda i, j: (last - RADIUS - j, i))

    loads[2].wait()
    lane = lax.broadcasted_iota(jnp.int32, (CELLS, features), 1)
    scaled = qbuf[...].astype(F32) * (HEAD_DIM ** (-0.5))
    for head in range(heads):
        own = lane // HEAD_DIM == head
        qstack[head * CELLS : (head + 1) * CELLS, :] = jnp.where(own, scaled, 0.0).astype(BF)

    pieces = 3
    piece = 4 * STRIP // pieces
    own_tops = []
    for head in range(heads):
        cols = slice(head * CELLS, (head + 1) * CELLS)
        score = dot_nt(kbuf[0:CELLS, :], qstack[cols, :])
        top = None
        for n in range(2):
            part = slice(n * 128, (n + 1) * 128)
            masked = score[part] + bias[part, :]
            weights[part, cols] = masked
            highest = jnp.max(masked.reshape(16, 8, CELLS), axis=0)
            top = highest if top is None else jnp.maximum(top, highest)
        own_tops.append(top)
    vt[:, 0:CELLS] = vbuf[0:CELLS, :].T
    loads[3].wait()
    gturned[0] = gbuf[0].T
    gathers[1].wait_recv()
    gathers[2].start()
    gturned[2] = gbuf[2].T
    gathers[0].wait_recv()
    gturned[1] = gbuf[1].T

    for copy in key_halos:
        copy.wait_recv()
    for head in range(heads):
        cols = slice(head * CELLS, (head + 1) * CELLS)
        score = dot_nt(kbuf[CELLS:EXT, :], qstack[cols, :])
        top = own_tops[head]
        for n in range(pieces):
            part = slice(CELLS + n * piece, CELLS + (n + 1) * piece)
            masked = score[n * piece : (n + 1) * piece] + bias[part, :]
            weights[part, cols] = masked
            top = jnp.maximum(top, jnp.max(masked.reshape(piece // 8, 8, CELLS), axis=0))
        top = jnp.max(top, axis=0, keepdims=True)
        total = None
        for n in range(5):
            part = slice(n * 128, (n + 1) * 128)
            raw = jnp.exp(weights[part, cols] - top)
            weights[part, cols] = raw
            summed = jnp.sum(raw.reshape(16, 8, CELLS), axis=0)
            total = summed if total is None else total + summed
        inverse = 1.0 / jnp.sum(total, axis=0, keepdims=True)
        for n in range(5):
            part = slice(n * 128, (n + 1) * 128)
            normal = weights[part, cols] * inverse
            weights[part, cols] = normal
            weights_bf[part, cols] = normal.astype(BF)
    gathers[2].wait_recv()
    gturned[3] = gbuf[3].T
    for copy in value_halos:
        copy.wait_recv()
    vt[:, CELLS:EXT] = vbuf[CELLS:EXT, :].T

    holders = (h, h1, h2, h3)
    half = features // 2
    per_slot = features // rows // nx * rows
    x_copies, y_copies = [], []
    for part in range(2):
        for head in range(part * heads // 2, (part + 1) * heads // 2):
            own_rows = slice(head * HEAD_DIM, (head + 1) * HEAD_DIM)
            att_t[own_rows, :] = dot(
                vt[own_rows, :], weights_bf[:, head * CELLS : (head + 1) * CELLS]
            )
        att_bf = att_t[part * half : (part + 1) * half, :].astype(BF)
        for slot in range(4):
            term = dot_nt(gturned[slot], att_bf)
            term = term.reshape(per_slot // rows, nx, rows, half)
            first = pl.multiple_of(holders[slot] * per_slot, per_slot)
            for xx in range(nx):
                xsend[part, xx, pl.ds(first, per_slot), :] = (
                    term[:, xx].reshape(per_slot, half).astype(BF)
                )
        x_copies.append(
            [
                pltpu.make_async_remote_copy(
                    src_ref=xsend.at[part, lax.rem(x + k, nx)],
                    dst_ref=xrecv.at[part, k - 1],
                    send_sem=x_send.at[part, k - 1],
                    recv_sem=x_recv.at[part, k - 1],
                    device_id=(x_peer(k), h),
                    device_id_type=MESH,
                )
                for k in range(1, nx)
            ]
        )
        for copy in x_copies[part]:
            copy.start()

    loads[4].wait()
    dout = None
    for slot in range(4):
        first = pl.multiple_of(holders[slot] * features, features)
        term = dot(gbuf[slot], wbuf[pl.ds(first, features), :])
        dout = term if dout is None else dout + term
    dout = dout.astype(BF).astype(F32)
    for head in range(heads):
        own = lane // HEAD_DIM == head
        dstack[head * CELLS : (head + 1) * CELLS, :] = jnp.where(own, dout, 0.0).astype(BF)

    def give_back(number, source, target, side):
        return pltpu.make_async_remote_copy(
            src_ref=source.at[side * STRIP : (side + 1) * STRIP],
            dst_ref=target.at[side * STRIP : (side + 1) * STRIP],
            send_sem=ret_send.at[number, side],
            recv_sem=ret_recv.at[number, side],
            device_id=(beside(side), h),
            device_id_type=MESH,
        )

    vback[...] = dot(weights_bf[CELLS:EXT, :], dstack[...]).astype(BF)
    value_returns = [give_back(1, vback, vreturned, side) for side in order]
    for copy in value_returns:
        copy.start()
    dout_t = dout.T
    row = lax.broadcasted_iota(jnp.int32, (features, CELLS), 0)
    product = dout_t * att_t[...]
    for head in range(heads):
        own = row // HEAD_DIM == head
        dturned[head * features : (head + 1) * features, :] = jnp.where(own, dout_t, 0.0).astype(BF)
    for head in range(heads):
        cols = slice(head * CELLS, (head + 1) * CELLS)
        own_rows = slice(head * HEAD_DIM, (head + 1) * HEAD_DIM)
        delta = jnp.sum(product[own_rows], axis=0, keepdims=True)
        grad_weight = dot(vbuf[...], dturned[head * features : (head + 1) * features, :])
        for n in range(5):
            part = slice(n * 128, (n + 1) * 128)
            dscore[part, cols] = (weights[part, cols] * (grad_weight[part] - delta)).astype(BF)
    kback[...] = dot(dscore[CELLS:EXT, :], qstack[...]).astype(BF)
    key_returns = [give_back(0, kback, kreturned, side) for side in order]
    for copy in key_returns:
        copy.start()

    block = nz * rows

    def sum_over_x(part):
        for copy in x_copies[part]:
            copy.wait_recv()
        total = xsend[part, x].astype(F32)
        for k in range(nx - 1):
            total = total + xrecv[part, k].astype(F32)
        ysum[part] = total.astype(BF)
        y_copies.append(
            [
                pltpu.make_async_remote_copy(
                    src_ref=ysum.at[
                        part, pl.ds(pl.multiple_of(lax.rem(y + k, ny) * block, block), block)
                    ],
                    dst_ref=yrecv.at[part, k - 1],
                    send_sem=y_send.at[part, k - 1],
                    recv_sem=y_recv.at[part, k - 1],
                    device_id=(y_peer(k), h),
                    device_id_type=MESH,
                )
                for k in range(1, ny)
            ]
        )
        for copy in y_copies[part]:
            copy.start()

    sum_over_x(0)
    centre_v[...] = dot(weights_bf[0:CELLS, :], dstack[...])
    sum_over_x(1)
    centre_k[...] = dot(dscore[0:CELLS, :], qstack[...])
    kt[...] = kbuf[...].T
    for head in range(heads):
        own_rows = slice(head * HEAD_DIM, (head + 1) * HEAD_DIM)
        gq_t[own_rows, :] = dot(kt[own_rows, :], dscore[:, head * CELLS : (head + 1) * CELLS])
    gq_out[...] = (gq_t[...].T * (HEAD_DIM ** (-0.5))).astype(BF)
    stores = [pltpu.make_async_copy(gq_out, gq_hbm, store_sem.at[0])]
    stores[0].start()

    for part in range(2):
        for copy in y_copies[part]:
            copy.wait_recv()
        total = ysum[part, pl.ds(pl.multiple_of(y * block, block), block), :].astype(F32)
        for k in range(ny - 1):
            total = total + yrecv[part, k].astype(F32)
        zsum[:, part * half : (part + 1) * half] = total
    z_copies = [
        pltpu.make_async_remote_copy(
            src_ref=zsum.at[pl.ds(pl.multiple_of(lax.rem(z + k, nz) * rows, rows), rows)],
            dst_ref=zrecv.at[k - 1],
            send_sem=z_send.at[k - 1],
            recv_sem=z_recv.at[k - 1],
            device_id=(z_peer(k), h),
            device_id_type=MESH,
        )
        for k in range(1, nz)
    ]
    for copy in z_copies:
        copy.start()

    for copy in value_returns:
        copy.wait_recv()
    gv_out[...] = (centre_v[...] + dot(pick_turned[...], vreturned[...])).astype(BF)
    stores.append(pltpu.make_async_copy(gv_out, gv_hbm, store_sem.at[2]))
    stores[1].start()
    for copy in key_returns:
        copy.wait_recv()
    gk_out[...] = (centre_k[...] + dot(pick_turned[...], kreturned[...])).astype(BF)
    stores.append(pltpu.make_async_copy(gk_out, gk_hbm, store_sem.at[1]))
    stores[2].start()

    for copy in z_copies:
        copy.wait_recv()
    total = zsum[pl.ds(pl.multiple_of(z * rows, rows), rows), :]
    for k in range(nz - 1):
        total = total + zrecv[k]
    gow_out[...] = total * (1.0 / math.sqrt(CELLS * tile_count))
    stores.append(pltpu.make_async_copy(gow_out, gow_hbm, store_sem.at[3]))
    stores[3].start()
    sent = key_halos + value_halos + gathers + key_returns + value_returns + z_copies
    for copy in sent + x_copies[0] + x_copies[1] + y_copies[0] + y_copies[1]:
        copy.wait_send()
    for store in stores:
        store.wait()


def handed_on(*refs):
    sources, targets, sems = refs[:4], refs[4:8], refs[8]
    copies = [pltpu.make_async_copy(a, b, sems.at[n]) for n, (a, b) in enumerate(zip(sources, targets))]
    for copy in copies:
        copy.start()
    for copy in copies:
        copy.wait()


def shards(queries, keys, values, grad_output, out_weight, rotations):
    tile_count = lax.axis_size("tile")
    tokens, features = queries.shape
    heads = features // HEAD_DIM
    width = out_weight.shape[0]
    rows = width // tile_count
    ny, nz, nx = tile_axes(tile_count)
    anywhere = pl.BlockSpec(memory_space=pl.ANY)
    out = jax.ShapeDtypeStruct((tokens, features), BF)
    dma = pltpu.SemaphoreType.DMA
    results = pl.pallas_call(
        functools.partial(kernel, tile_count),
        out_shape=(out, out, out, jax.ShapeDtypeStruct((rows, features), F32)),
        in_specs=[anywhere] * 5 + [pl.BlockSpec(memory_space=pltpu.SMEM)],
        out_specs=(pl.BlockSpec(memory_space=pltpu.VMEM),) * 4,
        scratch_shapes=[
            pltpu.VMEM((CELLS, features), BF),
            pltpu.VMEM((EXT, features), BF),
            pltpu.VMEM((EXT, features), BF),
            pltpu.VMEM((4, CELLS, features), BF),
            pltpu.VMEM((4, features, CELLS), BF),
            pltpu.VMEM((width, features), BF),
            pltpu.VMEM((4 * STRIP, CELLS), BF),
            pltpu.VMEM((CELLS, 4 * STRIP), BF),
            pltpu.VMEM((4 * STRIP, features), BF),
            pltpu.VMEM((4 * STRIP, features), BF),
            pltpu.VMEM((EXT, CELLS), F32),
            pltpu.VMEM((heads * CELLS, features), BF),
            pltpu.VMEM((features, EXT), BF),
            pltpu.VMEM((features, EXT), BF),
            pltpu.VMEM((EXT, heads * CELLS), F32),
            pltpu.VMEM((EXT, heads * CELLS), BF),
            pltpu.VMEM((EXT, heads * CELLS), BF),
            pltpu.VMEM((features, CELLS), F32),
            pltpu.VMEM((heads * CELLS, features), BF),
            pltpu.VMEM((heads * features, CELLS), BF),
            pltpu.VMEM((CELLS, features), F32),
            pltpu.VMEM((CELLS, features), F32),
            pltpu.VMEM((4 * STRIP, features), BF),
            pltpu.VMEM((4 * STRIP, features), BF),
            pltpu.VMEM((4 * STRIP, features), BF),
            pltpu.VMEM((4 * STRIP, features), BF),
            pltpu.VMEM((2, nx, width // nx, features // 2), BF),
            pltpu.VMEM((2, nx - 1, width // nx, features // 2), BF),
            pltpu.VMEM((2, width // nx, features // 2), BF),
            pltpu.VMEM((2, ny - 1, nz * rows, features // 2), BF),
            pltpu.VMEM((nz * rows, features), F32),
            pltpu.VMEM((nz - 1, rows, features), F32),
            pltpu.VMEM((CELLS, features), BF),
            pltpu.VMEM((CELLS, features), BF),
            pltpu.VMEM((CELLS, features), BF),
            pltpu.VMEM((rows, features), F32),
            pltpu.VMEM((features, CELLS), F32),
            dma((5,)),
            dma((4,)),
            dma((3,)),
            dma((3,)),
            dma((2, 4)),
            dma((2, 4)),
            dma((2, 4)),
            dma((2, 4)),
            dma((2, nx - 1)),
            dma((2, nx - 1)),
            dma((2, ny - 1)),
            dma((2, ny - 1)),
            dma((nz - 1,)),
            dma((nz - 1,)),
        ],
        compiler_params=pltpu.CompilerParams(collective_id=0, has_side_effects=True),
    )(queries, keys, values, grad_output, out_weight, rotations)
    return pl.pallas_call(
        handed_on,
        out_shape=(out, out, out, jax.ShapeDtypeStruct((rows, features), F32)),
        in_specs=[pl.BlockSpec(memory_space=pltpu.VMEM)] * 4,
        out_specs=(anywhere,) * 4,
        scratch_shapes=[dma((4,))],
    )(*results)


def solution(mesh):
    placed = (
        P("tile", "head"),
        P("tile", "head"),
        P("tile", "head"),
        P("tile", "head"),
        P(None, "head"),
        P("tile", None),
    )
    return jax.shard_map(
        shards,
        mesh=mesh,
        in_specs=placed,
        out_specs=(P("tile", "head"), P("tile", "head"), P("tile", "head"), P("tile", "head")),
        check_vma=False,
    )
```

```python
import functools
import math

import jax
import jax.numpy as jnp
from jax import lax
from jax.experimental import pallas as pl
from jax.experimental.pallas import tpu as pltpu
from jax.sharding import PartitionSpec as P

HEAD_DIM = 64
RADIUS = 6
SIDE = 16
CELLS = SIDE * SIDE
STRIP = RADIUS * SIDE
EXT = CELLS + 4 * STRIP
MESH = pl.DeviceIdType.MESH
BF = jnp.bfloat16
F32 = jnp.float32
NT = (((1,), (1,)), ((), ()))


def dot(a, b):
    return jnp.dot(a, b, preferred_element_type=F32)


def dot_nt(a, b):
    return lax.dot_general(a, b, NT, preferred_element_type=F32)


def tile_axes(tile_count):
    return {128: (8, 4, 4), 8: (2, 2, 2)}[tile_count]


def kernel(
    tile_count,
    q_hbm,
    k_hbm,
    v_hbm,
    g_hbm,
    w_hbm,
    rot_ref,
    gq_hbm,
    gk_hbm,
    gv_hbm,
    gow_hbm,
    qbuf,
    kbuf,
    vbuf,
    gbuf,
    gturned,
    wbuf,
    pick,
    pick_turned,
    kstrips,
    vstrips,
    bias,
    qstack,
    kt,
    vt,
    weights,
    weights_bf,
    dscore,
    att_t,
    dstack,
    dturned,
    centre_k,
    centre_v,
    kback,
    vback,
    kreturned,
    vreturned,
    xsend,
    xrecv,
    ysum,
    yrecv,
    zsum,
    zrecv,
    gq_out,
    gk_out,
    gv_out,
    gow_out,
    gq_t,
    load_sem,
    store_sem,
    ag_send,
    ag_recv,
    halo_send,
    halo_recv,
    ret_send,
    ret_recv,
    x_send,
    x_recv,
    y_send,
    y_recv,
    z_send,
    z_recv,
):
    ny, nz, nx = tile_axes(tile_count)
    features = q_hbm.shape[1]
    heads = features // HEAD_DIM
    rows = gow_hbm.shape[0]
    t = lax.axis_index("tile")
    h = lax.axis_index("head")
    x = lax.rem(t, nx)
    z = lax.rem(t // nx, nz)
    y = t // (nx * nz)
    h1 = h + 1 - 2 * lax.rem(h, 2)
    h2 = lax.rem(h + 2, 4)
    h3 = 3 - h

    def at_xyz(yy, zz, xx):
        return (yy * nz + zz) * nx + xx

    def x_peer(k):
        return at_xyz(y, z, lax.rem(x + k, nx))

    def y_peer(k):
        return at_xyz(lax.rem(y + k, ny), z, x)

    def z_peer(k):
        return at_xyz(y, lax.rem(z + k, nz), x)

    offsets = (-(tile_count // 4), 1, tile_count // 4, -1)

    def beside(side):
        return lax.rem(t + offsets[side] + tile_count, tile_count)

    loads = [
        pltpu.make_async_copy(k_hbm, kbuf.at[0:CELLS], load_sem.at[0]),
        pltpu.make_async_copy(q_hbm, qbuf, load_sem.at[2]),
        pltpu.make_async_copy(g_hbm, gbuf.at[0], load_sem.at[3]),
        pltpu.make_async_copy(w_hbm, wbuf, load_sem.at[4]),
    ]
    half = features // 2
    value_loads = [
        pltpu.make_async_copy(
            v_hbm.at[:, part * half : (part + 1) * half],
            vbuf.at[part, 0:CELLS],
            load_sem.at[(1, 5)[part]],
        )
        for part in range(2)
    ]
    barrier = pltpu.get_barrier_semaphore()
    peers = [(t, h1), (t, h2), (t, h3)]
    peers += [(beside(side), h) for side in range(4)]
    peers += [(y_peer(k), h) for k in range(1, ny)]
    peers += [(x_peer(k), h) for k in range(1, nx)]
    peers += [(z_peer(k), h) for k in range(1, nz)]
    for peer in peers:
        pl.semaphore_signal(barrier, inc=1, device_id=peer, device_id_type=MESH)
    for load in loads[:1] + value_loads + loads[1:]:
        load.start()

    starts, down, along = [], [], []
    for side in range(4):
        turn = lax.rem(side + 4 - rot_ref[0, (side + 2) % 4], 4)

        def choose(a, b, c, d, turn=turn):
            return jnp.where(turn == 0, a, jnp.where(turn == 1, b, jnp.where(turn == 2, c, d)))

        starts.append(choose(160, 5, 95, 250))
        down.append(choose(16, -1, -16, 1))
        along.append(choose(1, 16, -1, -16))
    place = lax.broadcasted_iota(jnp.int32, (STRIP, CELLS), 0)
    cell = lax.broadcasted_iota(jnp.int32, (STRIP, CELLS), 1)
    for side in range(4):
        target = starts[side] + down[side] * (place // SIDE) + along[side] * (place % SIDE)
        pick[side * STRIP : (side + 1) * STRIP, :] = jnp.where(cell == target, 1.0, 0.0).astype(BF)
    loads[0].wait()
    kstrips[...] = dot(pick[...], kbuf[0:CELLS, :]).astype(BF)
    for part in range(2):
        value_loads[part].wait()
        vstrips[part] = dot(pick[...], vbuf[part, 0:CELLS, :]).astype(BF)

    def halo(number, source, target, side):
        return pltpu.make_async_remote_copy(
            src_ref=source.at[side * STRIP : (side + 1) * STRIP],
            dst_ref=target.at[CELLS + side * STRIP : CELLS + (side + 1) * STRIP],
            send_sem=halo_send.at[number, side],
            recv_sem=halo_recv.at[number, side],
            device_id=(beside((side + 2) % 4), h),
            device_id_type=MESH,
        )

    order = (1, 3, 0, 2)
    key_halos = [halo(0, kstrips, kbuf, side) for side in order]
    value_halos = [
        [halo(1 + part, vstrips.at[part], vbuf.at[part], side) for side in order]
        for part in range(2)
    ]
    gathers = [
        pltpu.make_async_remote_copy(
            src_ref=source,
            dst_ref=gbuf.at[slot],
            send_sem=ag_send.at[slot - 1],
            recv_sem=ag_recv.at[slot - 1],
            device_id=(t, peer),
            device_id_type=MESH,
        )
        for slot, source, peer in ((1, g_hbm, h1), (2, g_hbm, h2), (3, gbuf.at[2], h1))
    ]
    pl.semaphore_wait(barrier, len(peers))
    for copy in key_halos:
        copy.start()
    gathers[0].start()
    for copy in value_halos[0]:
        copy.start()
    gathers[1].start()
    for copy in value_halos[1]:
        copy.start()

    cell_t = lax.broadcasted_iota(jnp.int32, (CELLS, 4 * STRIP), 0)
    place_t = lax.broadcasted_iota(jnp.int32, (CELLS, 4 * STRIP), 1)
    side_t = place_t // STRIP
    rest_t = place_t - side_t * STRIP

    def by_side(values):
        return jnp.where(
            side_t == 0,
            values[0],
            jnp.where(side_t == 1, values[1], jnp.where(side_t == 2, values[2], values[3])),
        )

    target_t = by_side(starts) + by_side(down) * (rest_t // SIDE) + by_side(along) * (rest_t % SIDE)
    pick_turned[...] = jnp.where(cell_t == target_t, 1.0, 0.0).astype(BF)

    def fill_bias(first, count, where_is):
        index = lax.broadcasted_iota(jnp.int32, (count, CELLS), 0)
        query = lax.broadcasted_iota(jnp.int32, (count, CELLS), 1)
        a, b = where_is(index // SIDE, index % SIDE)
        off_a = a - query // SIDE
        off_b = b - query % SIDE
        inside = (off_a >= 0) & (off_a <= 2 * RADIUS) & (off_b >= 0) & (off_b <= 2 * RADIUS)
        bias[first : first + count, :] = jnp.where(inside, 0.0, -1e30)

    last = SIDE + 2 * RADIUS - 1
    fill_bias(0, CELLS, lambda i, j: (i + RADIUS, j + RADIUS))
    fill_bias(CELLS, STRIP, lambda i, j: (i, RADIUS + j))
    fill_bias(CELLS + STRIP, STRIP, lambda i, j: (RADIUS + j, last - i))
    fill_bias(CELLS + 2 * STRIP, STRIP, lambda i, j: (last - i, last - RADIUS - j))
    fill_bias(CELLS + 3 * STRIP, STRIP, lambda i, j: (last - RADIUS - j, i))

    loads[1].wait()
    lane = lax.broadcasted_iota(jnp.int32, (CELLS, features), 1)
    scaled = qbuf[...].astype(F32) * (HEAD_DIM ** (-0.5))
    for head in range(heads):
        own = lane // HEAD_DIM == head
        qstack[head * CELLS : (head + 1) * CELLS, :] = jnp.where(own, scaled, 0.0).astype(BF)

    pieces = 3
    piece = 4 * STRIP // pieces
    own_tops = []
    for head in range(heads):
        cols = slice(head * CELLS, (head + 1) * CELLS)
        score = dot_nt(kbuf[0:CELLS, :], qstack[cols, :])
        top = None
        for n in range(2):
            part = slice(n * 128, (n + 1) * 128)
            masked = score[part] + bias[part, :]
            weights[part, cols] = masked
            highest = jnp.max(masked.reshape(16, 8, CELLS), axis=0)
            top = highest if top is None else jnp.maximum(top, highest)
        own_tops.append(top)
    for part in range(2):
        vt[part * half : (part + 1) * half, 0:CELLS] = vbuf[part, 0:CELLS, :].T
    loads[2].wait()
    gturned[0] = gbuf[0].T
    gathers[1].wait_recv()
    gathers[2].start()
    gturned[2] = gbuf[2].T
    gathers[0].wait_recv()
    gturned[1] = gbuf[1].T

    for copy in key_halos:
        copy.wait_recv()
    for head in range(heads):
        cols = slice(head * CELLS, (head + 1) * CELLS)
        score = dot_nt(kbuf[CELLS:EXT, :], qstack[cols, :])
        top = own_tops[head]
        for n in range(pieces):
            part = slice(CELLS + n * piece, CELLS + (n + 1) * piece)
            masked = score[n * piece : (n + 1) * piece] + bias[part, :]
            weights[part, cols] = masked
            top = jnp.maximum(top, jnp.max(masked.reshape(piece // 8, 8, CELLS), axis=0))
        top = jnp.max(top, axis=0, keepdims=True)
        total = None
        for n in range(5):
            part = slice(n * 128, (n + 1) * 128)
            raw = jnp.exp(weights[part, cols] - top)
            weights[part, cols] = raw
            summed = jnp.sum(raw.reshape(16, 8, CELLS), axis=0)
            total = summed if total is None else total + summed
        inverse = 1.0 / jnp.sum(total, axis=0, keepdims=True)
        for n in range(5):
            part = slice(n * 128, (n + 1) * 128)
            normal = weights[part, cols] * inverse
            weights[part, cols] = normal
            weights_bf[part, cols] = normal.astype(BF)
    gathers[2].wait_recv()
    gturned[3] = gbuf[3].T

    holders = (h, h1, h2, h3)
    per_slot = features // rows // nx * rows
    x_copies, y_copies = [], []
    for part in range(2):
        for copy in value_halos[part]:
            copy.wait_recv()
        vt[part * half : (part + 1) * half, CELLS:EXT] = vbuf[part, CELLS:EXT, :].T
        for head in range(part * heads // 2, (part + 1) * heads // 2):
            own_rows = slice(head * HEAD_DIM, (head + 1) * HEAD_DIM)
            att_t[own_rows, :] = dot(
                vt[own_rows, :], weights_bf[:, head * CELLS : (head + 1) * CELLS]
            )
        att_bf = att_t[part * half : (part + 1) * half, :].astype(BF)
        for slot in range(4):
            term = dot_nt(gturned[slot], att_bf)
            term = term.reshape(per_slot // rows, nx, rows, half)
            first = pl.multiple_of(holders[slot] * per_slot, per_slot)
            for xx in range(nx):
                xsend[part, xx, pl.ds(first, per_slot), :] = (
                    term[:, xx].reshape(per_slot, half).astype(BF)
                )
        x_copies.append(
            [
                pltpu.make_async_remote_copy(
                    src_ref=xsend.at[part, lax.rem(x + k, nx)],
                    dst_ref=xrecv.at[part, k - 1],
                    send_sem=x_send.at[part, k - 1],
                    recv_sem=x_recv.at[part, k - 1],
                    device_id=(x_peer(k), h),
                    device_id_type=MESH,
                )
                for k in range(1, nx)
            ]
        )
        for copy in x_copies[part]:
            copy.start()

    loads[3].wait()
    dout = None
    for slot in range(4):
        first = pl.multiple_of(holders[slot] * features, features)
        term = dot(gbuf[slot], wbuf[pl.ds(first, features), :])
        dout = term if dout is None else dout + term
    dout = dout.astype(BF).astype(F32)
    for head in range(heads):
        own = lane // HEAD_DIM == head
        dstack[head * CELLS : (head + 1) * CELLS, :] = jnp.where(own, dout, 0.0).astype(BF)

    def give_back(number, source, target, side):
        return pltpu.make_async_remote_copy(
            src_ref=source.at[side * STRIP : (side + 1) * STRIP],
            dst_ref=target.at[side * STRIP : (side + 1) * STRIP],
            send_sem=ret_send.at[number, side],
            recv_sem=ret_recv.at[number, side],
            device_id=(beside(side), h),
            device_id_type=MESH,
        )

    vback[...] = dot(weights_bf[CELLS:EXT, :], dstack[...]).astype(BF)
    value_returns = [give_back(1, vback, vreturned, side) for side in order]
    for copy in value_returns:
        copy.start()
    dout_t = dout.T
    row = lax.broadcasted_iota(jnp.int32, (half, CELLS), 0)
    product = dout_t * att_t[...]
    for head in range(heads):
        part = 2 * head // heads
        own = row // HEAD_DIM + part * half // HEAD_DIM == head
        dturned[head * half : (head + 1) * half, :] = jnp.where(
            own, dout_t[part * half : (part + 1) * half], 0.0
        ).astype(BF)
    for head in range(heads):
        cols = slice(head * CELLS, (head + 1) * CELLS)
        own_rows = slice(head * HEAD_DIM, (head + 1) * HEAD_DIM)
        delta = jnp.sum(product[own_rows], axis=0, keepdims=True)
        grad_weight = dot(vbuf[2 * head // heads], dturned[head * half : (head + 1) * half, :])
        for n in range(5):
            part = slice(n * 128, (n + 1) * 128)
            dscore[part, cols] = (weights[part, cols] * (grad_weight[part] - delta)).astype(BF)
    kback[...] = dot(dscore[CELLS:EXT, :], qstack[...]).astype(BF)
    key_returns = [give_back(0, kback, kreturned, side) for side in order]
    for copy in key_returns:
        copy.start()

    block = nz * rows

    def sum_over_x(part):
        for copy in x_copies[part]:
            copy.wait_recv()
        total = xsend[part, x].astype(F32)
        for k in range(nx - 1):
            total = total + xrecv[part, k].astype(F32)
        ysum[part] = total.astype(BF)
        y_copies.append(
            [
                pltpu.make_async_remote_copy(
                    src_ref=ysum.at[
                        part, pl.ds(pl.multiple_of(lax.rem(y + k, ny) * block, block), block)
                    ],
                    dst_ref=yrecv.at[part, k - 1],
                    send_sem=y_send.at[part, k - 1],
                    recv_sem=y_recv.at[part, k - 1],
                    device_id=(y_peer(k), h),
                    device_id_type=MESH,
                )
                for k in range(1, ny)
            ]
        )
        for copy in y_copies[part]:
            copy.start()

    sum_over_x(0)
    centre_v[...] = dot(weights_bf[0:CELLS, :], dstack[...])
    sum_over_x(1)
    centre_k[...] = dot(dscore[0:CELLS, :], qstack[...])
    kt[...] = kbuf[...].T
    for head in range(heads):
        own_rows = slice(head * HEAD_DIM, (head + 1) * HEAD_DIM)
        gq_t[own_rows, :] = dot(kt[own_rows, :], dscore[:, head * CELLS : (head + 1) * CELLS])
    gq_out[...] = (gq_t[...].T * (HEAD_DIM ** (-0.5))).astype(BF)
    stores = [pltpu.make_async_copy(gq_out, gq_hbm, store_sem.at[0])]
    stores[0].start()

    for part in range(2):
        for copy in y_copies[part]:
            copy.wait_recv()
        total = ysum[part, pl.ds(pl.multiple_of(y * block, block), block), :].astype(F32)
        for k in range(ny - 1):
            total = total + yrecv[part, k].astype(F32)
        zsum[:, part * half : (part + 1) * half] = total
    z_copies = [
        pltpu.make_async_remote_copy(
            src_ref=zsum.at[pl.ds(pl.multiple_of(lax.rem(z + k, nz) * rows, rows), rows)],
            dst_ref=zrecv.at[k - 1],
            send_sem=z_send.at[k - 1],
            recv_sem=z_recv.at[k - 1],
            device_id=(z_peer(k), h),
            device_id_type=MESH,
        )
        for k in range(1, nz)
    ]
    for copy in z_copies:
        copy.start()

    for copy in value_returns:
        copy.wait_recv()
    gv_out[...] = (centre_v[...] + dot(pick_turned[...], vreturned[...])).astype(BF)
    stores.append(pltpu.make_async_copy(gv_out, gv_hbm, store_sem.at[2]))
    stores[1].start()
    for copy in key_returns:
        copy.wait_recv()
    gk_out[...] = (centre_k[...] + dot(pick_turned[...], kreturned[...])).astype(BF)
    stores.append(pltpu.make_async_copy(gk_out, gk_hbm, store_sem.at[1]))
    stores[2].start()

    for copy in z_copies:
        copy.wait_recv()
    total = zsum[pl.ds(pl.multiple_of(z * rows, rows), rows), :]
    for k in range(nz - 1):
        total = total + zrecv[k]
    gow_out[...] = total * (1.0 / math.sqrt(CELLS * tile_count))
    stores.append(pltpu.make_async_copy(gow_out, gow_hbm, store_sem.at[3]))
    stores[3].start()
    sent = key_halos + value_halos[0] + value_halos[1] + gathers + key_returns + value_returns + z_copies
    for copy in sent + x_copies[0] + x_copies[1] + y_copies[0] + y_copies[1]:
        copy.wait_send()
    for store in stores:
        store.wait()


def handed_on(*refs):
    sources, targets, held, sems = refs[:4], refs[4:8], refs[8:12], refs[12]
    taken = [pltpu.make_async_copy(sources[n], held[n], sems.at[0, n]) for n in range(4)]
    given = [pltpu.make_async_copy(held[n], targets[n], sems.at[1, n]) for n in range(4)]
    for copy in taken:
        copy.start()
    for n in range(4):
        taken[n].wait()
        given[n].start()
    for copy in given:
        copy.wait()


def shards(queries, keys, values, grad_output, out_weight, rotations):
    tile_count = lax.axis_size("tile")
    tokens, features = queries.shape
    heads = features // HEAD_DIM
    width = out_weight.shape[0]
    rows = width // tile_count
    ny, nz, nx = tile_axes(tile_count)
    anywhere = pl.BlockSpec(memory_space=pl.ANY)
    out = jax.ShapeDtypeStruct((tokens, features), BF)
    dma = pltpu.SemaphoreType.DMA
    results = pl.pallas_call(
        functools.partial(kernel, tile_count),
        out_shape=(out, out, out, jax.ShapeDtypeStruct((rows, features), F32)),
        in_specs=[anywhere] * 5 + [pl.BlockSpec(memory_space=pltpu.SMEM)],
        out_specs=(pl.BlockSpec(memory_space=pltpu.VMEM),) * 4,
        scratch_shapes=[
            pltpu.VMEM((CELLS, features), BF),
            pltpu.VMEM((EXT, features), BF),
            pltpu.VMEM((2, EXT, features // 2), BF),
            pltpu.VMEM((4, CELLS, features), BF),
            pltpu.VMEM((4, features, CELLS), BF),
            pltpu.VMEM((width, features), BF),
            pltpu.VMEM((4 * STRIP, CELLS), BF),
            pltpu.VMEM((CELLS, 4 * STRIP), BF),
            pltpu.VMEM((4 * STRIP, features), BF),
            pltpu.VMEM((2, 4 * STRIP, features // 2), BF),
            pltpu.VMEM((EXT, CELLS), F32),
            pltpu.VMEM((heads * CELLS, features), BF),
            pltpu.VMEM((features, EXT), BF),
            pltpu.VMEM((features, EXT), BF),
            pltpu.VMEM((EXT, heads * CELLS), F32),
            pltpu.VMEM((EXT, heads * CELLS), BF),
            pltpu.VMEM((EXT, heads * CELLS), BF),
            pltpu.VMEM((features, CELLS), F32),
            pltpu.VMEM((heads * CELLS, features), BF),
            pltpu.VMEM((heads * features // 2, CELLS), BF),
            pltpu.VMEM((CELLS, features), F32),
            pltpu.VMEM((CELLS, features), F32),
            pltpu.VMEM((4 * STRIP, features), BF),
            pltpu.VMEM((4 * STRIP, features), BF),
            pltpu.VMEM((4 * STRIP, features), BF),
            pltpu.VMEM((4 * STRIP, features), BF),
            pltpu.VMEM((2, nx, width // nx, features // 2), BF),
            pltpu.VMEM((2, nx - 1, width // nx, features // 2), BF),
            pltpu.VMEM((2, width // nx, features // 2), BF),
            pltpu.VMEM((2, ny - 1, nz * rows, features // 2), BF),
            pltpu.VMEM((nz * rows, features), F32),
            pltpu.VMEM((nz - 1, rows, features), F32),
            pltpu.VMEM((CELLS, features), BF),
            pltpu.VMEM((CELLS, features), BF),
            pltpu.VMEM((CELLS, features), BF),
            pltpu.VMEM((rows, features), F32),
            pltpu.VMEM((features, CELLS), F32),
            dma((6,)),
            dma((4,)),
            dma((3,)),
            dma((3,)),
            dma((3, 4)),
            dma((3, 4)),
            dma((2, 4)),
            dma((2, 4)),
            dma((2, nx - 1)),
            dma((2, nx - 1)),
            dma((2, ny - 1)),
            dma((2, ny - 1)),
            dma((nz - 1,)),
            dma((nz - 1,)),
        ],
        compiler_params=pltpu.CompilerParams(collective_id=0, has_side_effects=True),
    )(queries, keys, values, grad_output, out_weight, rotations)
    return pl.pallas_call(
        handed_on,
        out_shape=(out, out, out, jax.ShapeDtypeStruct((rows, features), F32)),
        in_specs=[anywhere] * 4,
        out_specs=(anywhere,) * 4,
        scratch_shapes=[pltpu.VMEM((tokens, features), BF)] * 3
        + [pltpu.VMEM((rows, features), F32), dma((2, 4))],
    )(*results)


def solution(mesh):
    placed = (
        P("tile", "head"),
        P("tile", "head"),
        P("tile", "head"),
        P("tile", "head"),
        P(None, "head"),
        P("tile", None),
    )
    return jax.shard_map(
        shards,
        mesh=mesh,
        in_specs=placed,
        out_specs=(P("tile", "head"), P("tile", "head"), P("tile", "head"), P("tile", "head")),
        check_vma=False,
    )
```

```python
import functools
import math

import jax
import jax.numpy as jnp
from jax import lax
from jax.experimental import pallas as pl
from jax.experimental.pallas import tpu as pltpu
from jax.sharding import PartitionSpec as P

HEAD_DIM = 64
RADIUS = 6
SIDE = 16
CELLS = SIDE * SIDE
STRIP = RADIUS * SIDE
EXT = CELLS + 4 * STRIP
MESH = pl.DeviceIdType.MESH
BF = jnp.bfloat16
F32 = jnp.float32
NT = (((1,), (1,)), ((), ()))


def dot(a, b):
    return jnp.dot(a, b, preferred_element_type=F32)


def dot_nt(a, b):
    return lax.dot_general(a, b, NT, preferred_element_type=F32)


def tile_axes(tile_count):
    return {128: (8, 4, 4), 8: (2, 2, 2)}[tile_count]


def kernel(
    tile_count,
    q_hbm,
    k_hbm,
    v_hbm,
    g_hbm,
    w_hbm,
    rot_ref,
    gq_hbm,
    gk_hbm,
    gv_hbm,
    gow_hbm,
    qbuf,
    kbuf,
    vbuf,
    gbuf,
    gturned,
    wbuf,
    pick,
    pick_turned,
    kstrips,
    vstrips,
    bias,
    qstack,
    kt,
    vt,
    weights,
    weights_bf,
    dscore,
    att_t,
    dstack,
    dturned,
    centre_k,
    centre_v,
    kback,
    vback,
    kreturned,
    vreturned,
    xsend,
    xrecv,
    ysum,
    yrecv,
    zsum,
    zrecv,
    gq_out,
    gk_out,
    gv_out,
    gow_out,
    gq_t,
    load_sem,
    store_sem,
    ag_send,
    ag_recv,
    halo_send,
    halo_recv,
    ret_send,
    ret_recv,
    x_send,
    x_recv,
    y_send,
    y_recv,
    z_send,
    z_recv,
):
    ny, nz, nx = tile_axes(tile_count)
    features = q_hbm.shape[1]
    heads = features // HEAD_DIM
    rows = gow_hbm.shape[0]
    t = lax.axis_index("tile")
    h = lax.axis_index("head")
    x = lax.rem(t, nx)
    z = lax.rem(t // nx, nz)
    y = t // (nx * nz)
    h1 = h + 1 - 2 * lax.rem(h, 2)
    h2 = lax.rem(h + 2, 4)
    h3 = 3 - h

    def at_xyz(yy, zz, xx):
        return (yy * nz + zz) * nx + xx

    def x_peer(k):
        return at_xyz(y, z, lax.rem(x + k, nx))

    def y_peer(k):
        return at_xyz(lax.rem(y + k, ny), z, x)

    def z_peer(k):
        return at_xyz(y, lax.rem(z + k, nz), x)

    offsets = (-(tile_count // 4), 1, tile_count // 4, -1)

    def beside(side):
        return lax.rem(t + offsets[side] + tile_count, tile_count)

    loads = [
        pltpu.make_async_copy(k_hbm, kbuf.at[0:CELLS], load_sem.at[0]),
        pltpu.make_async_copy(q_hbm, qbuf, load_sem.at[2]),
        pltpu.make_async_copy(g_hbm, gbuf.at[0], load_sem.at[3]),
        pltpu.make_async_copy(w_hbm, wbuf, load_sem.at[4]),
    ]
    half = features // 2
    value_loads = [
        pltpu.make_async_copy(
            v_hbm.at[:, part * half : (part + 1) * half],
            vbuf.at[part, 0:CELLS],
            load_sem.at[(1, 5)[part]],
        )
        for part in range(2)
    ]
    barrier = pltpu.get_barrier_semaphore()
    peers = [(t, h1), (t, h2), (t, h3)]
    peers += [(beside(side), h) for side in range(4)]
    peers += [(y_peer(k), h) for k in range(1, ny)]
    peers += [(x_peer(k), h) for k in range(1, nx)]
    peers += [(z_peer(k), h) for k in range(1, nz)]
    for peer in peers:
        pl.semaphore_signal(barrier, inc=1, device_id=peer, device_id_type=MESH)
    for load in loads[:1] + value_loads + loads[1:]:
        load.start()

    starts, down, along = [], [], []
    for side in range(4):
        turn = lax.rem(side + 4 - rot_ref[0, (side + 2) % 4], 4)

        def choose(a, b, c, d, turn=turn):
            return jnp.where(turn == 0, a, jnp.where(turn == 1, b, jnp.where(turn == 2, c, d)))

        starts.append(choose(160, 5, 95, 250))
        down.append(choose(16, -1, -16, 1))
        along.append(choose(1, 16, -1, -16))
    place = lax.broadcasted_iota(jnp.int32, (STRIP, CELLS), 0)
    cell = lax.broadcasted_iota(jnp.int32, (STRIP, CELLS), 1)
    for side in range(4):
        target = starts[side] + down[side] * (place // SIDE) + along[side] * (place % SIDE)
        pick[side * STRIP : (side + 1) * STRIP, :] = jnp.where(cell == target, 1.0, 0.0).astype(BF)
    loads[0].wait()
    kstrips[...] = dot(pick[...], kbuf[0:CELLS, :]).astype(BF)
    for part in range(2):
        value_loads[part].wait()
        vstrips[part] = dot(pick[...], vbuf[part, 0:CELLS, :]).astype(BF)

    def halo(number, source, target, side):
        return pltpu.make_async_remote_copy(
            src_ref=source.at[side * STRIP : (side + 1) * STRIP],
            dst_ref=target.at[CELLS + side * STRIP : CELLS + (side + 1) * STRIP],
            send_sem=halo_send.at[number, side],
            recv_sem=halo_recv.at[number, side],
            device_id=(beside((side + 2) % 4), h),
            device_id_type=MESH,
        )

    order = (1, 3, 0, 2)
    key_halos = [halo(0, kstrips, kbuf, side) for side in order]
    value_halos = [
        [halo(1 + part, vstrips.at[part], vbuf.at[part], side) for side in order]
        for part in range(2)
    ]
    gathers = [
        pltpu.make_async_remote_copy(
            src_ref=source,
            dst_ref=gbuf.at[slot],
            send_sem=ag_send.at[slot - 1],
            recv_sem=ag_recv.at[slot - 1],
            device_id=(t, peer),
            device_id_type=MESH,
        )
        for slot, source, peer in ((1, g_hbm, h1), (2, g_hbm, h2), (3, gbuf.at[2], h1))
    ]
    pl.semaphore_wait(barrier, len(peers))
    for copy in key_halos:
        copy.start()
    gathers[0].start()
    for copy in value_halos[0]:
        copy.start()
    gathers[1].start()
    for copy in value_halos[1]:
        copy.start()

    cell_t = lax.broadcasted_iota(jnp.int32, (CELLS, 4 * STRIP), 0)
    place_t = lax.broadcasted_iota(jnp.int32, (CELLS, 4 * STRIP), 1)
    side_t = place_t // STRIP
    rest_t = place_t - side_t * STRIP

    def by_side(values):
        return jnp.where(
            side_t == 0,
            values[0],
            jnp.where(side_t == 1, values[1], jnp.where(side_t == 2, values[2], values[3])),
        )

    target_t = by_side(starts) + by_side(down) * (rest_t // SIDE) + by_side(along) * (rest_t % SIDE)
    pick_turned[...] = jnp.where(cell_t == target_t, 1.0, 0.0).astype(BF)

    def fill_bias(first, count, where_is):
        index = lax.broadcasted_iota(jnp.int32, (count, CELLS), 0)
        query = lax.broadcasted_iota(jnp.int32, (count, CELLS), 1)
        a, b = where_is(index // SIDE, index % SIDE)
        off_a = a - query // SIDE
        off_b = b - query % SIDE
        inside = (off_a >= 0) & (off_a <= 2 * RADIUS) & (off_b >= 0) & (off_b <= 2 * RADIUS)
        bias[first : first + count, :] = jnp.where(inside, 0.0, -1e30)

    last = SIDE + 2 * RADIUS - 1
    fill_bias(0, CELLS, lambda i, j: (i + RADIUS, j + RADIUS))
    fill_bias(CELLS, STRIP, lambda i, j: (i, RADIUS + j))
    fill_bias(CELLS + STRIP, STRIP, lambda i, j: (RADIUS + j, last - i))
    fill_bias(CELLS + 2 * STRIP, STRIP, lambda i, j: (last - i, last - RADIUS - j))
    fill_bias(CELLS + 3 * STRIP, STRIP, lambda i, j: (last - RADIUS - j, i))

    loads[1].wait()
    lane = lax.broadcasted_iota(jnp.int32, (CELLS, features), 1)
    scaled = qbuf[...].astype(F32) * (HEAD_DIM ** (-0.5))
    for head in range(heads):
        own = lane // HEAD_DIM == head
        qstack[head * CELLS : (head + 1) * CELLS, :] = jnp.where(own, scaled, 0.0).astype(BF)

    pieces = 3
    piece = 4 * STRIP // pieces
    own_tops = []
    for head in range(heads):
        cols = slice(head * CELLS, (head + 1) * CELLS)
        score = dot_nt(kbuf[0:CELLS, :], qstack[cols, :])
        top = None
        for n in range(2):
            part = slice(n * 128, (n + 1) * 128)
            masked = score[part] + bias[part, :]
            weights[part, cols] = masked
            highest = jnp.max(masked.reshape(16, 8, CELLS), axis=0)
            top = highest if top is None else jnp.maximum(top, highest)
        own_tops.append(top)
    for part in range(2):
        vt[part * half : (part + 1) * half, 0:CELLS] = vbuf[part, 0:CELLS, :].T
    loads[2].wait()
    gturned[0] = gbuf[0].T
    gathers[1].wait_recv()
    gathers[2].start()
    gturned[2] = gbuf[2].T
    gathers[0].wait_recv()
    gturned[1] = gbuf[1].T

    for copy in key_halos:
        copy.wait_recv()
    for head in range(heads):
        cols = slice(head * CELLS, (head + 1) * CELLS)
        score = dot_nt(kbuf[CELLS:EXT, :], qstack[cols, :])
        top = own_tops[head]
        for n in range(pieces):
            part = slice(CELLS + n * piece, CELLS + (n + 1) * piece)
            masked = score[n * piece : (n + 1) * piece] + bias[part, :]
            weights[part, cols] = masked
            top = jnp.maximum(top, jnp.max(masked.reshape(piece // 8, 8, CELLS), axis=0))
        top = jnp.max(top, axis=0, keepdims=True)
        total = None
        for n in range(5):
            part = slice(n * 128, (n + 1) * 128)
            raw = jnp.exp(weights[part, cols] - top)
            weights[part, cols] = raw
            summed = jnp.sum(raw.reshape(16, 8, CELLS), axis=0)
            total = summed if total is None else total + summed
        inverse = 1.0 / jnp.sum(total, axis=0, keepdims=True)
        for n in range(5):
            part = slice(n * 128, (n + 1) * 128)
            normal = weights[part, cols] * inverse
            weights[part, cols] = normal
            weights_bf[part, cols] = normal.astype(BF)
    gathers[2].wait_recv()
    gturned[3] = gbuf[3].T

    holders = (h, h1, h2, h3)
    per_slot = features // rows // nx * rows
    x_copies, y_copies = [], []
    for part in range(2):
        for copy in value_halos[part]:
            copy.wait_recv()
        vt[part * half : (part + 1) * half, CELLS:EXT] = vbuf[part, CELLS:EXT, :].T
        for head in range(part * heads // 2, (part + 1) * heads // 2):
            own_rows = slice(head * HEAD_DIM, (head + 1) * HEAD_DIM)
            att_t[own_rows, :] = dot(
                vt[own_rows, :], weights_bf[:, head * CELLS : (head + 1) * CELLS]
            )
        att_bf = att_t[part * half : (part + 1) * half, :].astype(BF)
        for slot in range(4):
            term = dot_nt(gturned[slot], att_bf)
            term = term.reshape(per_slot // rows, nx, rows, half)
            first = pl.multiple_of(holders[slot] * per_slot, per_slot)
            for xx in range(nx):
                xsend[part, xx, pl.ds(first, per_slot), :] = (
                    term[:, xx].reshape(per_slot, half).astype(BF)
                )
        x_copies.append(
            [
                pltpu.make_async_remote_copy(
                    src_ref=xsend.at[part, lax.rem(x + k, nx)],
                    dst_ref=xrecv.at[part, k - 1],
                    send_sem=x_send.at[part, k - 1],
                    recv_sem=x_recv.at[part, k - 1],
                    device_id=(x_peer(k), h),
                    device_id_type=MESH,
                )
                for k in sorted(range(1, nx), key=lambda k: -min(k, nx - k))
            ]
        )
        for copy in x_copies[part]:
            copy.start()

    loads[3].wait()
    dout = None
    for slot in range(4):
        first = pl.multiple_of(holders[slot] * features, features)
        term = dot(gbuf[slot], wbuf[pl.ds(first, features), :])
        dout = term if dout is None else dout + term
    dout = dout.astype(BF).astype(F32)
    for head in range(heads):
        own = lane // HEAD_DIM == head
        dstack[head * CELLS : (head + 1) * CELLS, :] = jnp.where(own, dout, 0.0).astype(BF)

    def give_back(number, source, target, side):
        return pltpu.make_async_remote_copy(
            src_ref=source.at[side * STRIP : (side + 1) * STRIP],
            dst_ref=target.at[side * STRIP : (side + 1) * STRIP],
            send_sem=ret_send.at[number, side],
            recv_sem=ret_recv.at[number, side],
            device_id=(beside(side), h),
            device_id_type=MESH,
        )

    vback[...] = dot(weights_bf[CELLS:EXT, :], dstack[...]).astype(BF)
    value_returns = [give_back(1, vback, vreturned, side) for side in order]
    for copy in value_returns:
        copy.start()
    dout_t = dout.T
    row = lax.broadcasted_iota(jnp.int32, (half, CELLS), 0)
    product = dout_t * att_t[...]
    for head in range(heads):
        part = 2 * head // heads
        own = row // HEAD_DIM + part * half // HEAD_DIM == head
        dturned[head * half : (head + 1) * half, :] = jnp.where(
            own, dout_t[part * half : (part + 1) * half], 0.0
        ).astype(BF)
    for head in range(heads):
        cols = slice(head * CELLS, (head + 1) * CELLS)
        own_rows = slice(head * HEAD_DIM, (head + 1) * HEAD_DIM)
        delta = jnp.sum(product[own_rows], axis=0, keepdims=True)
        grad_weight = dot(vbuf[2 * head // heads], dturned[head * half : (head + 1) * half, :])
        for n in range(5):
            part = slice(n * 128, (n + 1) * 128)
            dscore[part, cols] = (weights[part, cols] * (grad_weight[part] - delta)).astype(BF)
    kback[...] = dot(dscore[CELLS:EXT, :], qstack[...]).astype(BF)
    key_returns = [give_back(0, kback, kreturned, side) for side in order]
    for copy in key_returns:
        copy.start()

    block = nz * rows

    def sum_over_x(part):
        for copy in x_copies[part]:
            copy.wait_recv()
        total = xsend[part, x].astype(F32)
        for k in range(nx - 1):
            total = total + xrecv[part, k].astype(F32)
        ysum[part] = total.astype(BF)
        y_copies.append(
            [
                pltpu.make_async_remote_copy(
                    src_ref=ysum.at[
                        part, pl.ds(pl.multiple_of(lax.rem(y + k, ny) * block, block), block)
                    ],
                    dst_ref=yrecv.at[part, k - 1],
                    send_sem=y_send.at[part, k - 1],
                    recv_sem=y_recv.at[part, k - 1],
                    device_id=(y_peer(k), h),
                    device_id_type=MESH,
                )
                for k in sorted(range(1, ny), key=lambda k: -min(k, ny - k))
            ]
        )
        for copy in y_copies[part]:
            copy.start()

    sum_over_x(0)
    centre_v[...] = dot(weights_bf[0:CELLS, :], dstack[...])
    sum_over_x(1)
    centre_k[...] = dot(dscore[0:CELLS, :], qstack[...])
    kt[...] = kbuf[...].T
    for head in range(heads):
        own_rows = slice(head * HEAD_DIM, (head + 1) * HEAD_DIM)
        gq_t[own_rows, :] = dot(kt[own_rows, :], dscore[:, head * CELLS : (head + 1) * CELLS])
    gq_out[...] = (gq_t[...].T * (HEAD_DIM ** (-0.5))).astype(BF)
    stores = [pltpu.make_async_copy(gq_out, gq_hbm, store_sem.at[0])]
    stores[0].start()

    for part in range(2):
        for copy in y_copies[part]:
            copy.wait_recv()
        total = ysum[part, pl.ds(pl.multiple_of(y * block, block), block), :].astype(F32)
        for k in range(ny - 1):
            total = total + yrecv[part, k].astype(F32)
        zsum[:, part * half : (part + 1) * half] = total
    z_copies = [
        pltpu.make_async_remote_copy(
            src_ref=zsum.at[pl.ds(pl.multiple_of(lax.rem(z + k, nz) * rows, rows), rows)],
            dst_ref=zrecv.at[k - 1],
            send_sem=z_send.at[k - 1],
            recv_sem=z_recv.at[k - 1],
            device_id=(z_peer(k), h),
            device_id_type=MESH,
        )
        for k in sorted(range(1, nz), key=lambda k: -min(k, nz - k))
    ]
    for copy in z_copies:
        copy.start()

    for copy in value_returns:
        copy.wait_recv()
    gv_out[...] = (centre_v[...] + dot(pick_turned[...], vreturned[...])).astype(BF)
    stores.append(pltpu.make_async_copy(gv_out, gv_hbm, store_sem.at[2]))
    stores[1].start()
    for copy in key_returns:
        copy.wait_recv()
    gk_out[...] = (centre_k[...] + dot(pick_turned[...], kreturned[...])).astype(BF)
    stores.append(pltpu.make_async_copy(gk_out, gk_hbm, store_sem.at[1]))
    stores[2].start()

    for copy in z_copies:
        copy.wait_recv()
    total = zsum[pl.ds(pl.multiple_of(z * rows, rows), rows), :]
    for k in range(nz - 1):
        total = total + zrecv[k]
    gow_out[...] = total * (1.0 / math.sqrt(CELLS * tile_count))
    stores.append(pltpu.make_async_copy(gow_out, gow_hbm, store_sem.at[3]))
    stores[3].start()
    sent = key_halos + value_halos[0] + value_halos[1] + gathers + key_returns + value_returns + z_copies
    for copy in sent + x_copies[0] + x_copies[1] + y_copies[0] + y_copies[1]:
        copy.wait_send()
    for store in stores:
        store.wait()


def handed_on(*refs):
    sources, targets, held, sems = refs[:4], refs[4:8], refs[8:12], refs[12]
    taken = [pltpu.make_async_copy(sources[n], held[n], sems.at[0, n]) for n in range(4)]
    given = [pltpu.make_async_copy(held[n], targets[n], sems.at[1, n]) for n in range(4)]
    for copy in taken:
        copy.start()
    for n in range(4):
        taken[n].wait()
        given[n].start()
    for copy in given:
        copy.wait()


def shards(queries, keys, values, grad_output, out_weight, rotations):
    tile_count = lax.axis_size("tile")
    tokens, features = queries.shape
    heads = features // HEAD_DIM
    width = out_weight.shape[0]
    rows = width // tile_count
    ny, nz, nx = tile_axes(tile_count)
    anywhere = pl.BlockSpec(memory_space=pl.ANY)
    out = jax.ShapeDtypeStruct((tokens, features), BF)
    dma = pltpu.SemaphoreType.DMA
    results = pl.pallas_call(
        functools.partial(kernel, tile_count),
        out_shape=(out, out, out, jax.ShapeDtypeStruct((rows, features), F32)),
        in_specs=[anywhere] * 5 + [pl.BlockSpec(memory_space=pltpu.SMEM)],
        out_specs=(pl.BlockSpec(memory_space=pltpu.VMEM),) * 4,
        scratch_shapes=[
            pltpu.VMEM((CELLS, features), BF),
            pltpu.VMEM((EXT, features), BF),
            pltpu.VMEM((2, EXT, features // 2), BF),
            pltpu.VMEM((4, CELLS, features), BF),
            pltpu.VMEM((4, features, CELLS), BF),
            pltpu.VMEM((width, features), BF),
            pltpu.VMEM((4 * STRIP, CELLS), BF),
            pltpu.VMEM((CELLS, 4 * STRIP), BF),
            pltpu.VMEM((4 * STRIP, features), BF),
            pltpu.VMEM((2, 4 * STRIP, features // 2), BF),
            pltpu.VMEM((EXT, CELLS), F32),
            pltpu.VMEM((heads * CELLS, features), BF),
            pltpu.VMEM((features, EXT), BF),
            pltpu.VMEM((features, EXT), BF),
            pltpu.VMEM((EXT, heads * CELLS), F32),
            pltpu.VMEM((EXT, heads * CELLS), BF),
            pltpu.VMEM((EXT, heads * CELLS), BF),
            pltpu.VMEM((features, CELLS), F32),
            pltpu.VMEM((heads * CELLS, features), BF),
            pltpu.VMEM((heads * features // 2, CELLS), BF),
            pltpu.VMEM((CELLS, features), F32),
            pltpu.VMEM((CELLS, features), F32),
            pltpu.VMEM((4 * STRIP, features), BF),
            pltpu.VMEM((4 * STRIP, features), BF),
            pltpu.VMEM((4 * STRIP, features), BF),
            pltpu.VMEM((4 * STRIP, features), BF),
            pltpu.VMEM((2, nx, width // nx, features // 2), BF),
            pltpu.VMEM((2, nx - 1, width // nx, features // 2), BF),
            pltpu.VMEM((2, width // nx, features // 2), BF),
            pltpu.VMEM((2, ny - 1, nz * rows, features // 2), BF),
            pltpu.VMEM((nz * rows, features), F32),
            pltpu.VMEM((nz - 1, rows, features), F32),
            pltpu.VMEM((CELLS, features), BF),
            pltpu.VMEM((CELLS, features), BF),
            pltpu.VMEM((CELLS, features), BF),
            pltpu.VMEM((rows, features), F32),
            pltpu.VMEM((features, CELLS), F32),
            dma((6,)),
            dma((4,)),
            dma((3,)),
            dma((3,)),
            dma((3, 4)),
            dma((3, 4)),
            dma((2, 4)),
            dma((2, 4)),
            dma((2, nx - 1)),
            dma((2, nx - 1)),
            dma((2, ny - 1)),
            dma((2, ny - 1)),
            dma((nz - 1,)),
            dma((nz - 1,)),
        ],
        compiler_params=pltpu.CompilerParams(collective_id=0, has_side_effects=True),
    )(queries, keys, values, grad_output, out_weight, rotations)
    return pl.pallas_call(
        handed_on,
        out_shape=(out, out, out, jax.ShapeDtypeStruct((rows, features), F32)),
        in_specs=[anywhere] * 4,
        out_specs=(anywhere,) * 4,
        scratch_shapes=[pltpu.VMEM((tokens, features), BF)] * 3
        + [pltpu.VMEM((rows, features), F32), dma((2, 4))],
    )(*results)


def solution(mesh):
    placed = (
        P("tile", "head"),
        P("tile", "head"),
        P("tile", "head"),
        P("tile", "head"),
        P(None, "head"),
        P("tile", None),
    )
    return jax.shard_map(
        shards,
        mesh=mesh,
        in_specs=placed,
        out_specs=(P("tile", "head"), P("tile", "head"), P("tile", "head"), P("tile", "head")),
        check_vma=False,
    )
```

```python
import functools
import math

import jax
import jax.numpy as jnp
from jax import lax
from jax.experimental import pallas as pl
from jax.experimental.pallas import tpu as pltpu
from jax.sharding import PartitionSpec as P

HEAD_DIM = 64
RADIUS = 6
SIDE = 16
CELLS = SIDE * SIDE
STRIP = RADIUS * SIDE
EXT = CELLS + 4 * STRIP
MESH = pl.DeviceIdType.MESH
BF = jnp.bfloat16
F32 = jnp.float32
NT = (((1,), (1,)), ((), ()))


def dot(a, b):
    return jnp.dot(a, b, preferred_element_type=F32)


def dot_nt(a, b):
    return lax.dot_general(a, b, NT, preferred_element_type=F32)


def tile_axes(tile_count):
    return {128: (8, 4, 4), 8: (2, 2, 2)}[tile_count]


def kernel(
    tile_count,
    q_hbm,
    k_hbm,
    v_hbm,
    g_hbm,
    w_hbm,
    rot_ref,
    gq_hbm,
    gk_hbm,
    gv_hbm,
    gow_hbm,
    qbuf,
    kbuf,
    vbuf,
    gbuf,
    gturned,
    wbuf,
    pick,
    pick_turned,
    kstrips,
    vstrips,
    bias,
    qstack,
    kt,
    vt,
    weights,
    weights_bf,
    dscore,
    att_t,
    dstack,
    dturned,
    centre_k,
    centre_v,
    kback,
    vback,
    kreturned,
    vreturned,
    xsend,
    xrecv,
    ysum,
    yrecv,
    zsum,
    zrecv,
    gq_out,
    gk_out,
    gv_out,
    gow_out,
    gq_t,
    load_sem,
    store_sem,
    ag_send,
    ag_recv,
    halo_send,
    halo_recv,
    ret_send,
    ret_recv,
    x_send,
    x_recv,
    y_send,
    y_recv,
    z_send,
    z_recv,
):
    ny, nz, nx = tile_axes(tile_count)
    features = q_hbm.shape[1]
    heads = features // HEAD_DIM
    rows = gow_hbm.shape[0]
    t = lax.axis_index("tile")
    h = lax.axis_index("head")
    x = lax.rem(t, nx)
    z = lax.rem(t // nx, nz)
    y = t // (nx * nz)
    h1 = h + 1 - 2 * lax.rem(h, 2)
    h2 = lax.rem(h + 2, 4)
    h3 = 3 - h

    def at_xyz(yy, zz, xx):
        return (yy * nz + zz) * nx + xx

    def x_peer(k):
        return at_xyz(y, z, lax.rem(x + k, nx))

    def y_peer(k):
        return at_xyz(lax.rem(y + k, ny), z, x)

    def z_peer(k):
        return at_xyz(y, lax.rem(z + k, nz), x)

    offsets = (-(tile_count // 4), 1, tile_count // 4, -1)

    def beside(side):
        return lax.rem(t + offsets[side] + tile_count, tile_count)

    loads = [
        pltpu.make_async_copy(k_hbm, kbuf.at[0:CELLS], load_sem.at[0]),
        pltpu.make_async_copy(q_hbm, qbuf, load_sem.at[2]),
        pltpu.make_async_copy(g_hbm, gbuf.at[0], load_sem.at[3]),
        pltpu.make_async_copy(w_hbm, wbuf, load_sem.at[4]),
    ]
    half = features // 2
    value_loads = [
        pltpu.make_async_copy(
            v_hbm.at[:, part * half : (part + 1) * half],
            vbuf.at[part, 0:CELLS],
            load_sem.at[(1, 5)[part]],
        )
        for part in range(2)
    ]
    barrier = pltpu.get_barrier_semaphore()
    peers = [(t, h1), (t, h2), (t, h3)]
    peers += [(beside(side), h) for side in range(4)]
    peers += [(y_peer(k), h) for k in range(1, ny)]
    peers += [(x_peer(k), h) for k in range(1, nx)]
    peers += [(z_peer(k), h) for k in range(1, nz)]
    for peer in peers:
        pl.semaphore_signal(barrier, inc=1, device_id=peer, device_id_type=MESH)
    for load in loads[:1] + value_loads + loads[1:]:
        load.start()

    starts, down, along = [], [], []
    for side in range(4):
        turn = lax.rem(side + 4 - rot_ref[0, (side + 2) % 4], 4)

        def choose(a, b, c, d, turn=turn):
            return jnp.where(turn == 0, a, jnp.where(turn == 1, b, jnp.where(turn == 2, c, d)))

        starts.append(choose(160, 5, 95, 250))
        down.append(choose(16, -1, -16, 1))
        along.append(choose(1, 16, -1, -16))
    place = lax.broadcasted_iota(jnp.int32, (STRIP, CELLS), 0)
    cell = lax.broadcasted_iota(jnp.int32, (STRIP, CELLS), 1)
    for side in range(4):
        target = starts[side] + down[side] * (place // SIDE) + along[side] * (place % SIDE)
        pick[side * STRIP : (side + 1) * STRIP, :] = jnp.where(cell == target, 1.0, 0.0).astype(BF)
    loads[0].wait()
    kstrips[...] = dot(pick[...], kbuf[0:CELLS, :]).astype(BF)
    for part in range(2):
        value_loads[part].wait()
        vstrips[part] = dot(pick[...], vbuf[part, 0:CELLS, :]).astype(BF)

    def halo(number, source, target, side):
        return pltpu.make_async_remote_copy(
            src_ref=source.at[side * STRIP : (side + 1) * STRIP],
            dst_ref=target.at[CELLS + side * STRIP : CELLS + (side + 1) * STRIP],
            send_sem=halo_send.at[number, side],
            recv_sem=halo_recv.at[number, side],
            device_id=(beside((side + 2) % 4), h),
            device_id_type=MESH,
        )

    order = (1, 3, 0, 2)
    key_halos = [halo(0, kstrips, kbuf, side) for side in order]
    value_halos = [
        [halo(1 + part, vstrips.at[part], vbuf.at[part], side) for side in order]
        for part in range(2)
    ]
    gathers = [
        pltpu.make_async_remote_copy(
            src_ref=source,
            dst_ref=gbuf.at[slot],
            send_sem=ag_send.at[slot - 1],
            recv_sem=ag_recv.at[slot - 1],
            device_id=(t, peer),
            device_id_type=MESH,
        )
        for slot, source, peer in ((1, g_hbm, h1), (2, g_hbm, h2), (3, gbuf.at[2], h1))
    ]
    pl.semaphore_wait(barrier, len(peers))
    for copy in key_halos:
        copy.start()
    gathers[0].start()
    for copy in value_halos[0]:
        copy.start()
    gathers[1].start()
    for copy in value_halos[1]:
        copy.start()

    cell_t = lax.broadcasted_iota(jnp.int32, (CELLS, 4 * STRIP), 0)
    place_t = lax.broadcasted_iota(jnp.int32, (CELLS, 4 * STRIP), 1)
    side_t = place_t // STRIP
    rest_t = place_t - side_t * STRIP

    def by_side(values):
        return jnp.where(
            side_t == 0,
            values[0],
            jnp.where(side_t == 1, values[1], jnp.where(side_t == 2, values[2], values[3])),
        )

    target_t = by_side(starts) + by_side(down) * (rest_t // SIDE) + by_side(along) * (rest_t % SIDE)
    pick_turned[...] = jnp.where(cell_t == target_t, 1.0, 0.0).astype(BF)

    def fill_bias(first, count, where_is):
        index = lax.broadcasted_iota(jnp.int32, (count, CELLS), 0)
        query = lax.broadcasted_iota(jnp.int32, (count, CELLS), 1)
        a, b = where_is(index // SIDE, index % SIDE)
        off_a = a - query // SIDE
        off_b = b - query % SIDE
        inside = (off_a >= 0) & (off_a <= 2 * RADIUS) & (off_b >= 0) & (off_b <= 2 * RADIUS)
        bias[first : first + count, :] = jnp.where(inside, 0.0, -1e30)

    last = SIDE + 2 * RADIUS - 1
    fill_bias(0, CELLS, lambda i, j: (i + RADIUS, j + RADIUS))
    fill_bias(CELLS, STRIP, lambda i, j: (i, RADIUS + j))
    fill_bias(CELLS + STRIP, STRIP, lambda i, j: (RADIUS + j, last - i))
    fill_bias(CELLS + 2 * STRIP, STRIP, lambda i, j: (last - i, last - RADIUS - j))
    fill_bias(CELLS + 3 * STRIP, STRIP, lambda i, j: (last - RADIUS - j, i))

    loads[1].wait()
    lane = lax.broadcasted_iota(jnp.int32, (CELLS, features), 1)
    scaled = qbuf[...].astype(F32) * (HEAD_DIM ** (-0.5))
    for head in range(heads):
        own = lane // HEAD_DIM == head
        qstack[head * CELLS : (head + 1) * CELLS, :] = jnp.where(own, scaled, 0.0).astype(BF)

    pieces = 3
    piece = 4 * STRIP // pieces
    own_tops = []
    for head in range(heads):
        cols = slice(head * CELLS, (head + 1) * CELLS)
        score = dot_nt(kbuf[0:CELLS, :], qstack[cols, :])
        top = None
        for n in range(2):
            part = slice(n * 128, (n + 1) * 128)
            masked = score[part] + bias[part, :]
            weights[part, cols] = masked
            highest = jnp.max(masked.reshape(16, 8, CELLS), axis=0)
            top = highest if top is None else jnp.maximum(top, highest)
        own_tops.append(top)
    for part in range(2):
        vt[part * half : (part + 1) * half, 0:CELLS] = vbuf[part, 0:CELLS, :].T
    loads[2].wait()
    gturned[0] = gbuf[0].T
    gathers[1].wait_recv()
    gathers[2].start()
    gturned[2] = gbuf[2].T
    gathers[0].wait_recv()
    gturned[1] = gbuf[1].T

    for copy in key_halos:
        copy.wait_recv()
    for head in range(heads):
        cols = slice(head * CELLS, (head + 1) * CELLS)
        score = dot_nt(kbuf[CELLS:EXT, :], qstack[cols, :])
        top = own_tops[head]
        for n in range(pieces):
            part = slice(CELLS + n * piece, CELLS + (n + 1) * piece)
            masked = score[n * piece : (n + 1) * piece] + bias[part, :]
            weights[part, cols] = masked
            top = jnp.maximum(top, jnp.max(masked.reshape(piece // 8, 8, CELLS), axis=0))
        top = jnp.max(top, axis=0, keepdims=True)
        total = None
        for n in range(5):
            part = slice(n * 128, (n + 1) * 128)
            raw = jnp.exp(weights[part, cols] - top)
            weights[part, cols] = raw
            summed = jnp.sum(raw.reshape(16, 8, CELLS), axis=0)
            total = summed if total is None else total + summed
        inverse = 1.0 / jnp.sum(total, axis=0, keepdims=True)
        for n in range(5):
            part = slice(n * 128, (n + 1) * 128)
            normal = weights[part, cols] * inverse
            weights[part, cols] = normal
            weights_bf[part, cols] = normal.astype(BF)
    gathers[2].wait_recv()
    gturned[3] = gbuf[3].T

    holders = (h, h1, h2, h3)
    per_slot = features // rows // nx * rows
    x_copies, y_copies = [], []
    for part in range(2):
        for copy in value_halos[part]:
            copy.wait_recv()
        vt[part * half : (part + 1) * half, CELLS:EXT] = vbuf[part, CELLS:EXT, :].T
        for head in range(part * heads // 2, (part + 1) * heads // 2):
            own_rows = slice(head * HEAD_DIM, (head + 1) * HEAD_DIM)
            att_t[own_rows, :] = dot(
                vt[own_rows, :], weights_bf[:, head * CELLS : (head + 1) * CELLS]
            )
        att_bf = att_t[part * half : (part + 1) * half, :].astype(BF)
        for slot in range(4):
            term = dot_nt(gturned[slot], att_bf)
            term = term.reshape(per_slot // rows, nx, rows, half)
            first = pl.multiple_of(holders[slot] * per_slot, per_slot)
            for xx in range(nx):
                xsend[part, xx, pl.ds(first, per_slot), :] = (
                    term[:, xx].reshape(per_slot, half).astype(BF)
                )
        x_copies.append(
            [
                pltpu.make_async_remote_copy(
                    src_ref=xsend.at[part, lax.rem(x + k, nx)],
                    dst_ref=xrecv.at[part, k - 1],
                    send_sem=x_send.at[part, k - 1],
                    recv_sem=x_recv.at[part, k - 1],
                    device_id=(x_peer(k), h),
                    device_id_type=MESH,
                )
                for k in sorted(range(1, nx), key=lambda k: -min(k, nx - k))
            ]
        )
        for copy in x_copies[part]:
            copy.start()

    loads[3].wait()
    dout = None
    for slot in range(4):
        first = pl.multiple_of(holders[slot] * features, features)
        term = dot(gbuf[slot], wbuf[pl.ds(first, features), :])
        dout = term if dout is None else dout + term
    dout = dout.astype(BF).astype(F32)
    for head in range(heads):
        own = lane // HEAD_DIM == head
        dstack[head * CELLS : (head + 1) * CELLS, :] = jnp.where(own, dout, 0.0).astype(BF)

    def give_back(number, source, target, side):
        return pltpu.make_async_remote_copy(
            src_ref=source.at[side * STRIP : (side + 1) * STRIP],
            dst_ref=target.at[side * STRIP : (side + 1) * STRIP],
            send_sem=ret_send.at[number, side],
            recv_sem=ret_recv.at[number, side],
            device_id=(beside(side), h),
            device_id_type=MESH,
        )

    vback[...] = dot(weights_bf[CELLS:EXT, :], dstack[...]).astype(BF)
    value_returns = [give_back(1, vback, vreturned, side) for side in order]
    for copy in value_returns:
        copy.start()
    dout_t = dout.T
    row = lax.broadcasted_iota(jnp.int32, (half, CELLS), 0)
    product = dout_t * att_t[...]
    for head in range(heads):
        part = 2 * head // heads
        own = row // HEAD_DIM + part * half // HEAD_DIM == head
        dturned[head * half : (head + 1) * half, :] = jnp.where(
            own, dout_t[part * half : (part + 1) * half], 0.0
        ).astype(BF)
    for head in range(heads):
        cols = slice(head * CELLS, (head + 1) * CELLS)
        own_rows = slice(head * HEAD_DIM, (head + 1) * HEAD_DIM)
        delta = jnp.sum(product[own_rows], axis=0, keepdims=True)
        grad_weight = dot(vbuf[2 * head // heads], dturned[head * half : (head + 1) * half, :])
        for n in range(5):
            part = slice(n * 128, (n + 1) * 128)
            dscore[part, cols] = (weights[part, cols] * (grad_weight[part] - delta)).astype(BF)
    key_returns = [give_back(0, kback, kreturned, side) for side in order]
    for copy, side in zip(key_returns, order):
        own = slice(side * STRIP, (side + 1) * STRIP)
        kback[own, :] = dot(
            dscore[CELLS + side * STRIP : CELLS + (side + 1) * STRIP, :], qstack[...]
        ).astype(BF)
        copy.start()

    block = nz * rows

    def sum_over_x(part):
        for copy in x_copies[part]:
            copy.wait_recv()
        total = xsend[part, x].astype(F32)
        for k in range(nx - 1):
            total = total + xrecv[part, k].astype(F32)
        ysum[part] = total.astype(BF)
        y_copies.append(
            [
                pltpu.make_async_remote_copy(
                    src_ref=ysum.at[
                        part, pl.ds(pl.multiple_of(lax.rem(y + k, ny) * block, block), block)
                    ],
                    dst_ref=yrecv.at[part, k - 1],
                    send_sem=y_send.at[part, k - 1],
                    recv_sem=y_recv.at[part, k - 1],
                    device_id=(y_peer(k), h),
                    device_id_type=MESH,
                )
                for k in sorted(range(1, ny), key=lambda k: -min(k, ny - k))
            ]
        )
        for copy in y_copies[part]:
            copy.start()

    sum_over_x(0)
    centre_v[...] = dot(weights_bf[0:CELLS, :], dstack[...])
    sum_over_x(1)
    centre_k[...] = dot(dscore[0:CELLS, :], qstack[...])
    kt[...] = kbuf[...].T
    for head in range(heads):
        own_rows = slice(head * HEAD_DIM, (head + 1) * HEAD_DIM)
        gq_t[own_rows, :] = dot(kt[own_rows, :], dscore[:, head * CELLS : (head + 1) * CELLS])
    gq_out[...] = (gq_t[...].T * (HEAD_DIM ** (-0.5))).astype(BF)
    stores = [pltpu.make_async_copy(gq_out, gq_hbm, store_sem.at[0])]
    stores[0].start()

    for part in range(2):
        for copy in y_copies[part]:
            copy.wait_recv()
        total = ysum[part, pl.ds(pl.multiple_of(y * block, block), block), :].astype(F32)
        for k in range(ny - 1):
            total = total + yrecv[part, k].astype(F32)
        zsum[:, part * half : (part + 1) * half] = total
    z_copies = [
        pltpu.make_async_remote_copy(
            src_ref=zsum.at[pl.ds(pl.multiple_of(lax.rem(z + k, nz) * rows, rows), rows)],
            dst_ref=zrecv.at[k - 1],
            send_sem=z_send.at[k - 1],
            recv_sem=z_recv.at[k - 1],
            device_id=(z_peer(k), h),
            device_id_type=MESH,
        )
        for k in sorted(range(1, nz), key=lambda k: -min(k, nz - k))
    ]
    for copy in z_copies:
        copy.start()

    for copy in value_returns:
        copy.wait_recv()
    gv_out[...] = (centre_v[...] + dot(pick_turned[...], vreturned[...])).astype(BF)
    stores.append(pltpu.make_async_copy(gv_out, gv_hbm, store_sem.at[2]))
    stores[1].start()
    for copy in key_returns:
        copy.wait_recv()
    gk_out[...] = (centre_k[...] + dot(pick_turned[...], kreturned[...])).astype(BF)
    stores.append(pltpu.make_async_copy(gk_out, gk_hbm, store_sem.at[1]))
    stores[2].start()

    for copy in z_copies:
        copy.wait_recv()
    total = zsum[pl.ds(pl.multiple_of(z * rows, rows), rows), :]
    for k in range(nz - 1):
        total = total + zrecv[k]
    gow_out[...] = total * (1.0 / math.sqrt(CELLS * tile_count))
    stores.append(pltpu.make_async_copy(gow_out, gow_hbm, store_sem.at[3]))
    stores[3].start()
    sent = key_halos + value_halos[0] + value_halos[1] + gathers + key_returns + value_returns + z_copies
    for copy in sent + x_copies[0] + x_copies[1] + y_copies[0] + y_copies[1]:
        copy.wait_send()
    for store in stores:
        store.wait()


def handed_on(*refs):
    sources, targets, held, sems = refs[:4], refs[4:8], refs[8:12], refs[12]
    taken = [pltpu.make_async_copy(sources[n], held[n], sems.at[0, n]) for n in range(4)]
    given = [pltpu.make_async_copy(held[n], targets[n], sems.at[1, n]) for n in range(4)]
    for copy in taken:
        copy.start()
    for n in range(4):
        taken[n].wait()
        given[n].start()
    for copy in given:
        copy.wait()


def shards(queries, keys, values, grad_output, out_weight, rotations):
    tile_count = lax.axis_size("tile")
    tokens, features = queries.shape
    heads = features // HEAD_DIM
    width = out_weight.shape[0]
    rows = width // tile_count
    ny, nz, nx = tile_axes(tile_count)
    anywhere = pl.BlockSpec(memory_space=pl.ANY)
    out = jax.ShapeDtypeStruct((tokens, features), BF)
    dma = pltpu.SemaphoreType.DMA
    results = pl.pallas_call(
        functools.partial(kernel, tile_count),
        out_shape=(out, out, out, jax.ShapeDtypeStruct((rows, features), F32)),
        in_specs=[anywhere] * 5 + [pl.BlockSpec(memory_space=pltpu.SMEM)],
        out_specs=(pl.BlockSpec(memory_space=pltpu.VMEM),) * 4,
        scratch_shapes=[
            pltpu.VMEM((CELLS, features), BF),
            pltpu.VMEM((EXT, features), BF),
            pltpu.VMEM((2, EXT, features // 2), BF),
            pltpu.VMEM((4, CELLS, features), BF),
            pltpu.VMEM((4, features, CELLS), BF),
            pltpu.VMEM((width, features), BF),
            pltpu.VMEM((4 * STRIP, CELLS), BF),
            pltpu.VMEM((CELLS, 4 * STRIP), BF),
            pltpu.VMEM((4 * STRIP, features), BF),
            pltpu.VMEM((2, 4 * STRIP, features // 2), BF),
            pltpu.VMEM((EXT, CELLS), F32),
            pltpu.VMEM((heads * CELLS, features), BF),
            pltpu.VMEM((features, EXT), BF),
            pltpu.VMEM((features, EXT), BF),
            pltpu.VMEM((EXT, heads * CELLS), F32),
            pltpu.VMEM((EXT, heads * CELLS), BF),
            pltpu.VMEM((EXT, heads * CELLS), BF),
            pltpu.VMEM((features, CELLS), F32),
            pltpu.VMEM((heads * CELLS, features), BF),
            pltpu.VMEM((heads * features // 2, CELLS), BF),
            pltpu.VMEM((CELLS, features), F32),
            pltpu.VMEM((CELLS, features), F32),
            pltpu.VMEM((4 * STRIP, features), BF),
            pltpu.VMEM((4 * STRIP, features), BF),
            pltpu.VMEM((4 * STRIP, features), BF),
            pltpu.VMEM((4 * STRIP, features), BF),
            pltpu.VMEM((2, nx, width // nx, features // 2), BF),
            pltpu.VMEM((2, nx - 1, width // nx, features // 2), BF),
            pltpu.VMEM((2, width // nx, features // 2), BF),
            pltpu.VMEM((2, ny - 1, nz * rows, features // 2), BF),
            pltpu.VMEM((nz * rows, features), F32),
            pltpu.VMEM((nz - 1, rows, features), F32),
            pltpu.VMEM((CELLS, features), BF),
            pltpu.VMEM((CELLS, features), BF),
            pltpu.VMEM((CELLS, features), BF),
            pltpu.VMEM((rows, features), F32),
            pltpu.VMEM((features, CELLS), F32),
            dma((6,)),
            dma((4,)),
            dma((3,)),
            dma((3,)),
            dma((3, 4)),
            dma((3, 4)),
            dma((2, 4)),
            dma((2, 4)),
            dma((2, nx - 1)),
            dma((2, nx - 1)),
            dma((2, ny - 1)),
            dma((2, ny - 1)),
            dma((nz - 1,)),
            dma((nz - 1,)),
        ],
        compiler_params=pltpu.CompilerParams(collective_id=0, has_side_effects=True),
    )(queries, keys, values, grad_output, out_weight, rotations)
    return pl.pallas_call(
        handed_on,
        out_shape=(out, out, out, jax.ShapeDtypeStruct((rows, features), F32)),
        in_specs=[anywhere] * 4,
        out_specs=(anywhere,) * 4,
        scratch_shapes=[pltpu.VMEM((tokens, features), BF)] * 3
        + [pltpu.VMEM((rows, features), F32), dma((2, 4))],
    )(*results)


def solution(mesh):
    placed = (
        P("tile", "head"),
        P("tile", "head"),
        P("tile", "head"),
        P("tile", "head"),
        P(None, "head"),
        P("tile", None),
    )
    return jax.shard_map(
        shards,
        mesh=mesh,
        in_specs=placed,
        out_specs=(P("tile", "head"), P("tile", "head"), P("tile", "head"), P("tile", "head")),
        check_vma=False,
    )
```
